32 devices in a mesh: fsdp: 8 (over z, x), pipe: 2 (over core), dp: 2 (over y).
Axes of the slice: x: 2, y: 2, z: 4, core: 2. Of those that a mesh axis runs over, the one named last changes fastest.
Arguments:
- video_tokens: bfloat16 [2, 1024, 2560], P('dp', 'fsdp'), may hold values from -6 to 6
- cached_out: bfloat16 [2, 2, 1024, 2560], P('pipe', 'dp', 'fsdp'), may hold values from -6 to 6
- fresh_mask: int32 [2, 2, 1024], P('pipe', 'dp', 'fsdp'), may hold values from 0 to 1, as said below
- timestep: int32 [2], P('dp'), may hold values from 0 to 49
- up_weight: bfloat16 [2, 7168, 2560], P('pipe', 'fsdp'), may hold values from -0.125 to 0.125
- down_weight: bfloat16 [2, 7168, 2560], P('pipe', 'fsdp'), may hold values from -0.0625 to 0.0625
- router_in: bfloat16 [2, 2560, 256], P('pipe', 'fsdp'), may hold values from -0.125 to 0.125
- router_bias: float32 [2, 50, 256], P('pipe'), may hold values from -6 to 6
- router_out: float32 [2, 256], P('pipe'), may hold values from -0.375 to 0.375
- out_cotangent: bfloat16 [2, 1024, 2560], P('dp', 'fsdp'), may hold values from -0.119628906 to 0.119628906
Outputs:
- blended: bfloat16 [2, 2, 1024, 2560], P('pipe', 'dp', 'fsdp')
- grad_router_in: float32 [2, 2560, 256], P('pipe', 'fsdp')
- grad_router_bias: float32 [2, 50, 256], P('pipe')
- grad_router_out: float32 [2, 256], P('pipe')
The draws below stay inside these ranges and needn't reach their ends.
Inputs may be any that keep to these rules, and one draw needn't show every extreme that they name: `fresh_mask`: for each section and video, the 128 consecutive tokens of one index of fsdp hold 1 to 2 ones, and some index holds exactly 2.
All inputs are finite; a program needn't handle non-finite values.
Results may differ from the reference program's by a relative error of at most 0.023.
Values may be sent and summed in bfloat16 or wider, within the bound.
A program may use at most 64 MiB of HBM per device.

```python
import jax
import jax.numpy as jnp
from jax import lax

D = 2560
FF = 7168
RH = 256
STEPS = 50
FRESH = 2
TOK_DEV = 128
TOKENS = 1024
VIDEOS = 2
N_FSDP = 8
N_DP = 2


def draw_fresh_mask(key, part):
    block_count = TOKENS // TOK_DEV
    key_count = jax.random.fold_in(key, 11)
    key_full = jax.random.fold_in(key, 12)
    key_order = jax.random.fold_in(key, 13)
    counts = jax.random.randint(key_count, (2, VIDEOS, block_count), FRESH // 2, FRESH + 1)
    full_block = jax.random.randint(key_full, (2, VIDEOS), 0, block_count)
    counts = jnp.where(jnp.arange(block_count)[None, None, :] == full_block[:, :, None], FRESH, counts)
    scores = jax.random.randint(key_order, (2, VIDEOS, block_count, TOK_DEV), 0, 1 << 20) * TOK_DEV + jnp.arange(TOK_DEV)[None, None, None, :]
    ranks = jnp.argsort(jnp.argsort(scores, axis=3), axis=3)
    chosen = (ranks < counts[:, :, :, None]).astype(jnp.int32)
    return chosen.reshape(2, VIDEOS, TOKENS)


def block_scale(stream_key, extent, cuts, low, top_value):
    factor_of, own = 1.0, jax.random.fold_in(stream_key, 6)
    for dim, blocks in cuts:
        draws = jnp.exp(jax.random.uniform(jax.random.fold_in(own, dim), (blocks,), jnp.float32, low / len(cuts), top_value / len(cuts)))
        factor_of = factor_of * jnp.repeat(draws, extent[dim] // blocks).reshape([-1 if axis == dim else 1 for axis in range(len(extent))])
    return factor_of


def scatter_about(key, extent, spread, limit, shards=(), held_as=jnp.bfloat16):
    factor_of = block_scale(key, extent, shards, -0.22, 0.18) if shards else 1.0
    entries = jax.random.normal(key, extent, jnp.float32) * spread * factor_of
    return jnp.minimum(jnp.maximum(entries, -limit), limit).astype(held_as)


def setup_inputs(seed: int = 0) -> dict:
    splits = jax.random.split(jax.random.key(seed), 11)
    video_tokens = scatter_about(splits[0], (VIDEOS, TOKENS, D), 1.0, 6.0, ((0, 2), (1, 8)))
    cached_out = scatter_about(splits[1], (2, VIDEOS, TOKENS, D), 1.0, 6.0, ((0, 2), (1, 2), (2, 8)))
    fresh_mask = draw_fresh_mask(jax.random.fold_in(splits[10], 71), 0)
    timestep = jax.random.randint(splits[3], (VIDEOS,), 0, STEPS).astype(jnp.int32)
    up_weight = scatter_about(splits[4], (2, FF, D), D ** -0.5, 0.125, ((0, 2), (1, 8)))
    down_weight = scatter_about(splits[5], (2, FF, D), FF ** -0.5, 0.0625, ((0, 2), (1, 8)))
    router_in = scatter_about(splits[6], (2, D, RH), D ** -0.5, 0.125, ((0, 2), (1, 8)))
    router_bias = scatter_about(splits[7], (2, STEPS, RH), 1.0, 6.0, ((0, 2),), jnp.float32)
    router_out = scatter_about(splits[8], (2, RH), RH ** -0.5, 0.375, ((0, 2),), jnp.float32)
    out_cotangent = scatter_about(splits[9], (VIDEOS, TOKENS, D), 0.02, 0.119628906, ((0, 2), (1, 8)))
    return dict(video_tokens=video_tokens, cached_out=cached_out, fresh_mask=fresh_mask, timestep=timestep, up_weight=up_weight, down_weight=down_weight, router_in=router_in, router_bias=router_bias, router_out=router_out, out_cotangent=out_cotangent)


layer_eps = 1e-06
gelu_scale = 0.7978845608028654
gelu_cubic = 0.044715

def gelu_tanh(values):
    inner_arg = gelu_scale * (values + gelu_cubic * values * values * values)
    return 0.5 * values * (1.0 + jnp.tanh(inner_arg))

def gelu_slope(values):
    inner_arg = gelu_scale * (values + gelu_cubic * values * values * values)
    tanh_val = jnp.tanh(inner_arg)
    return 0.5 * (1.0 + tanh_val) + 0.5 * values * (1.0 - tanh_val * tanh_val) * gelu_scale * (1.0 + 3.0 * gelu_cubic * values * values)

def normalize(inputs):
    values = inputs.astype(jnp.float32)
    center = values - lax.optimization_barrier(jnp.mean(values, axis=1, keepdims=True))
    inv_std = lax.rsqrt(lax.optimization_barrier(jnp.mean(center * center, axis=1, keepdims=True)) + layer_eps)
    return (center * inv_std, inv_std)

def normalize_back(scaled, inv_std, grads):
    return inv_std * (grads - lax.optimization_barrier(jnp.mean(grads, axis=1, keepdims=True)) - scaled * lax.optimization_barrier(jnp.mean(grads * scaled, axis=1, keepdims=True)))

def pack_index(mask_row):
    blocks_mask = mask_row.reshape(N_FSDP, TOK_DEV)
    order = jnp.argsort(1 - blocks_mask, axis=1, stable=True)[:, :FRESH].astype(jnp.int32)
    index = order + (jnp.arange(N_FSDP, dtype=jnp.int32) * TOK_DEV)[:, None]
    live = (jnp.arange(FRESH)[None, :] < lax.optimization_barrier(jnp.sum(blocks_mask, axis=1))[:, None]).astype(jnp.float32)
    return (index.reshape(-1).astype(jnp.int32), live.reshape(-1))

def block_terms(left, weight):
    rows = left.shape[0]
    parts = jnp.transpose(left.reshape(rows, N_FSDP, FF // N_FSDP), (1, 0, 2))
    weight_parts = weight.reshape(N_FSDP, FF // N_FSDP, D)

    def one_block(pair):
        return jnp.dot(pair[0], pair[1], preferred_element_type=jnp.float32)
    return lax.map(one_block, (parts, weight_parts))

def section_forward(rows_in, cached_rows, live_rows, bias_row, w_up, w_down, r_in, r_out):
    scaled, inv_std = normalize(rows_in)
    normed = scaled.astype(jnp.bfloat16)
    pre_act = jnp.dot(normed, w_up.T, preferred_element_type=jnp.float32)
    hid_act = gelu_tanh(pre_act).astype(jnp.bfloat16)
    blocks = block_terms(hid_act, w_down)
    block_sum = lax.optimization_barrier(jnp.sum(blocks.astype(jnp.bfloat16).astype(jnp.float32), axis=0))
    fresh_out = rows_in.astype(jnp.float32) + block_sum
    router_pre = jnp.dot(normed, r_in, preferred_element_type=jnp.float32) + bias_row[None, :]
    gate = jax.nn.sigmoid(jnp.dot(gelu_tanh(router_pre), r_out, precision=lax.Precision.HIGHEST))
    delta = live_rows[:, None] * gate[:, None] * (fresh_out - cached_rows)
    return (delta, (scaled, inv_std, normed, pre_act, router_pre, gate, fresh_out, cached_rows))

def router_back(stored, live_rows, cotangent, r_out):
    scaled, inv_std, normed, pre_act, router_pre, gate, fresh_out, cached_f = stored
    gate_grad = lax.optimization_barrier(jnp.sum(cotangent * live_rows[:, None] * (fresh_out - cached_f), axis=1))
    fresh_grad = cotangent * (live_rows * gate)[:, None]
    logit_grad = gate_grad * gate * (1.0 - gate)
    out_grad = jnp.dot(logit_grad, gelu_tanh(router_pre), precision=lax.Precision.HIGHEST)
    hidden_grad = logit_grad[:, None] * r_out[None, :] * gelu_slope(router_pre)
    hidden_b = hidden_grad.astype(jnp.bfloat16)
    in_grad = jnp.dot(normed.T, hidden_b, preferred_element_type=jnp.float32)
    bias_sum = lax.optimization_barrier(jnp.sum(hidden_grad, axis=0))
    return (fresh_grad, hidden_b, in_grad, bias_sum, out_grad)

def block_back(stored, fresh_grad, hidden_b, w_up, w_down, r_in):
    scaled, inv_std, normed, pre_act, router_pre, gate, fresh_out, cached_f = stored
    rows = fresh_grad.shape[0]
    fresh_b = fresh_grad.astype(jnp.bfloat16)
    act_grad = jnp.dot(fresh_b, w_down.T, preferred_element_type=jnp.float32)
    pre_grad = (act_grad * gelu_slope(pre_act)).astype(jnp.bfloat16)
    blocks = block_terms(pre_grad, w_up)
    router_term = jnp.dot(hidden_b, r_in.T, preferred_element_type=jnp.float32)
    placed = router_term.reshape(rows, N_FSDP, D // N_FSDP)[None] * jnp.eye(N_FSDP, dtype=jnp.float32)[:, None, :, None]
    blocks = blocks + placed.reshape(N_FSDP, rows, D)
    normed_grad = lax.optimization_barrier(jnp.sum(blocks.astype(jnp.bfloat16).astype(jnp.float32), axis=0))
    return fresh_grad + normalize_back(scaled, inv_std, normed_grad)

def reference(video_tokens, cached_out, fresh_mask, timestep, up_weight, down_weight, router_in, router_bias, router_out, out_cotangent):
    first_out = []
    second_out = []
    in_grads = [jnp.zeros((D, RH), jnp.float32), jnp.zeros((D, RH), jnp.float32)]
    bias_grads = [jnp.zeros((STEPS, RH), jnp.float32), jnp.zeros((STEPS, RH), jnp.float32)]
    out_grads = [jnp.zeros((RH,), jnp.float32), jnp.zeros((RH,), jnp.float32)]
    for video_index in range(N_DP):
        hot_step = (jnp.arange(STEPS) == timestep[video_index]).astype(jnp.float32)
        bias_first = jnp.dot(hot_step, router_bias[0], precision=lax.Precision.HIGHEST)
        bias_second = jnp.dot(hot_step, router_bias[1], precision=lax.Precision.HIGHEST)
        index_first, live_first = pack_index(fresh_mask[0, video_index])
        index_second, live_second = pack_index(fresh_mask[1, video_index])
        cached_first = cached_out[0, video_index].astype(jnp.float32)
        cached_second = cached_out[1, video_index].astype(jnp.float32)
        delta_first, stored_first = section_forward(video_tokens[video_index][index_first], cached_first[index_first], live_first, bias_first, up_weight[0], down_weight[0], router_in[0], router_out[0])
        out_first = cached_first.at[index_first].add(delta_first).astype(jnp.bfloat16)
        delta_second, stored_second = section_forward(out_first[index_second], cached_second[index_second], live_second, bias_second, up_weight[1], down_weight[1], router_in[1], router_out[1])
        out_second = cached_second.at[index_second].add(delta_second).astype(jnp.bfloat16)
        cot_second = out_cotangent[video_index].astype(jnp.float32)[index_second]
        fresh_grad, hidden_b, in_second, bias_second_sum, out_second_grad = router_back(stored_second, live_second, cot_second, router_out[1])
        input_grad = block_back(stored_second, fresh_grad, hidden_b, up_weight[1], down_weight[1], router_in[1])
        full_grad = jnp.zeros((TOKENS, D), jnp.float32).at[index_second].add(input_grad)
        cot_first = full_grad[index_first]
        unused_grad, unused_hidden, in_first, bias_first_sum, out_first_grad = router_back(stored_first, live_first, cot_first, router_out[0])
        in_grads = [in_grads[0] + in_first, in_grads[1] + in_second]
        bias_grads = [bias_grads[0] + hot_step[:, None] * bias_first_sum[None, :], bias_grads[1] + hot_step[:, None] * bias_second_sum[None, :]]
        out_grads = [out_grads[0] + out_first_grad, out_grads[1] + out_second_grad]
        first_out.append(out_first)
        second_out.append(out_second)
    blended = jnp.stack([jnp.stack(first_out), jnp.stack(second_out)])
    return (blended, jnp.stack(in_grads), jnp.stack(bias_grads), jnp.stack(out_grads))
```

```python
import functools

import jax
import jax.numpy as jnp
from jax import lax
from jax.experimental import pallas as pl
from jax.experimental.pallas import tpu as pltpu
from jax.sharding import PartitionSpec as P

FRESH = 2

layer_eps = 1e-06
gelu_scale = 0.7978845608028654
gelu_cubic = 0.044715
F32 = jnp.float32
BF16 = jnp.bfloat16
MESH = pl.DeviceIdType.MESH


def gelu_both(values):
    inner_arg = gelu_scale * (values + gelu_cubic * values * values * values)
    tanh_val = jnp.tanh(inner_arg)
    gelu = 0.5 * values * (1.0 + tanh_val)
    slope = 0.5 * (1.0 + tanh_val) + 0.5 * values * (1.0 - tanh_val * tanh_val) * gelu_scale * (
        1.0 + 3.0 * gelu_cubic * values * values
    )
    return gelu, slope


def normalize(values):
    center = values - jnp.mean(values, axis=1, keepdims=True)
    inv_std = lax.rsqrt(jnp.mean(center * center, axis=1, keepdims=True) + layer_eps)
    return center * inv_std, inv_std


def normalize_back(scaled, inv_std, grads):
    return inv_std * (
        grads
        - jnp.mean(grads, axis=1, keepdims=True)
        - scaled * jnp.mean(grads * scaled, axis=1, keepdims=True)
    )


def dot_nn(left, right):
    return jnp.dot(left, right, preferred_element_type=F32)


def dot_nt(left, right):
    return lax.dot_general(left, right, (((1,), (1,)), ((), ())), preferred_element_type=F32)


def dot_tn(left, right):
    return lax.dot_general(left, right, (((0,), (0,)), ((), ())), preferred_element_type=F32)


def kernel(
    n,
    n_dp,
    tokens_hbm,
    cached_hbm,
    mask_ref,
    step_ref,
    up_hbm,
    down_hbm,
    rin_ref,
    bias_ref,
    rout_ref,
    cot_hbm,
    blended_hbm,
    in_grad_ref,
    bias_grad_ref,
    out_grad_ref,
    up,
    down,
    first,
    cached,
    blend,
    sel,
    psel,
    xin,
    in1,
    x32,
    pre,
    send1,
    recv1,
    delta,
    delta_in,
    factors,
    factors_in,
    fgrad,
    total,
    send2,
    recv2,
    cols,
    gmsg,
    gfirst,
    hid,
    load_sem,
    sel_sems,
    x_send,
    x_recv,
    r1_send,
    r1_recv,
    aux_sems,
    f_send,
    f_recv,
    r2_send,
    r2_recv,
    c_send,
    c_recv,
    g_send,
    g_recv,
    out_sem,
):
    k = lax.axis_index("fsdp")
    p = lax.axis_index("pipe")
    v = lax.axis_index("dp")
    is0 = p == 0
    is1 = p == 1
    dim = up.shape[1]
    rh = rin_ref.shape[1]
    cols_n = rin_ref.shape[0]
    rows = n * FRESH

    load_rows = pltpu.make_async_copy(tokens_hbm, first, load_sem.at[0])
    load_cot = pltpu.make_async_copy(cot_hbm, first, load_sem.at[0])
    load_cached = pltpu.make_async_copy(cached_hbm, cached, load_sem.at[1])
    load_up = pltpu.make_async_copy(up_hbm, up, load_sem.at[2])
    load_down = pltpu.make_async_copy(down_hbm, down, load_sem.at[3])

    @pl.when(is0)
    def _():
        load_rows.start()

    @pl.when(is1)
    def _():
        load_cot.start()

    load_cached.start()
    load_up.start()
    load_down.start()

    barrier = pltpu.get_barrier_semaphore()
    count = n * 2 * n_dp
    flat = (k * 2 + p) * n_dp + v

    @pl.loop(1, count)
    def _(i):
        other = lax.rem(flat + i, count)
        pl.semaphore_signal(
            barrier,
            inc=1,
            device_id={
                "fsdp": other // (2 * n_dp),
                "pipe": lax.rem(other // n_dp, 2),
                "dp": lax.rem(other, n_dp),
            },
            device_id_type=MESH,
        )

    toks = mask_ref.shape[1]
    lane = lax.broadcasted_iota(jnp.int32, (1, toks), 1).astype(F32)
    fresh = mask_ref[...] > 0
    low = jnp.min(jnp.where(fresh, lane, float(toks)), axis=1, keepdims=True)
    high = jnp.max(jnp.where(fresh, lane, -1.0), axis=1, keepdims=True)
    hot_low = jnp.where(lane == low, 1.0, 0.0)
    hot_high = jnp.where(jnp.logical_and(lane == high, high > low), 1.0, 0.0)
    row8 = lax.broadcasted_iota(jnp.int32, (8, toks), 0)
    hot = jnp.where(row8 == 0, hot_low, jnp.where(row8 == 1, hot_high, 0.0))
    sel[...] = hot
    hot_b = hot.astype(BF16)
    live = jnp.sum(hot, axis=1, keepdims=True)[:FRESH]

    load_rows.wait()
    picked = dot_nn(hot_b, first[...])[:FRESH]

    @pl.when(is0)
    def _():
        xin[k] = picked.astype(BF16)

    pl.semaphore_wait(barrier, count - 1)

    def peer_copy(src, dst, send_sem, recv_sem, j, **where):
        return pltpu.make_async_remote_copy(
            src_ref=src,
            dst_ref=dst,
            send_sem=send_sem,
            recv_sem=recv_sem,
            device_id={"fsdp": j, "pipe": p, "dp": v, **where},
            device_id_type=MESH,
        )

    @pl.when(is0)
    def _():
        @pl.loop(1, n)
        def _(i):
            j = lax.rem(k + i, n)
            peer_copy(xin.at[k], xin.at[k], x_send.at[j], x_recv.at[k], j).start()

    sel_copy = peer_copy(sel, psel, sel_sems.at[0], sel_sems.at[1], k, pipe=1 - p)
    sel_copy.start()
    load_cached.wait()
    cached_rows = dot_nn(hot_b, cached[...])[:FRESH]
    sel_copy.wait()
    other_hot = psel[...]
    same_0 = jnp.sum(other_hot[:FRESH] * hot[0:1], axis=1, keepdims=True)
    same_1 = jnp.sum(other_hot[:FRESH] * hot[1:2], axis=1, keepdims=True)
    other_rows = dot_nn(other_hot.astype(BF16), cached[...])[:FRESH]
    step_val = jnp.full((1, rh), step_ref[0], jnp.int32)
    step_row = lax.broadcasted_iota(jnp.int32, bias_ref.shape, 0)
    bias_row = jnp.sum(jnp.where(step_row == step_ref[0], bias_ref[...], 0.0), axis=0, keepdims=True)
    load_up.wait()
    load_down.wait()

    @pl.when(is0)
    def _():
        @pl.loop(1, n)
        def _(i):
            j = lax.rem(k + i, n)
            peer_copy(xin.at[j], xin.at[j], x_send.at[j], x_recv.at[j], j).wait()

    @pl.when(is1)
    def _():
        @pl.loop(0, n)
        def _(j):
            peer_copy(xin.at[j], xin.at[j], x_send.at[j], x_recv.at[j], j, pipe=0).wait_recv()

    for j in range(n):
        x32[j * FRESH : (j + 1) * FRESH, :] = xin[j].astype(F32)
    scaled_all, _ = normalize(x32[...])
    x32[...] = scaled_all
    normed = scaled_all.astype(BF16)
    for j in range(n):

        @pl.when(k == j)
        def _():
            cols[v] = x32[:, j * cols_n : (j + 1) * cols_n].astype(BF16)

    router_part = dot_nn(cols[v], rin_ref[...])
    pre_act = dot_nt(normed, up[...])
    act, slope = gelu_both(pre_act)
    pre[...] = slope
    term = dot_nn(act.astype(BF16), down[...])
    for j in range(n):
        send1[j, :, :dim] = term[j * FRESH : (j + 1) * FRESH].astype(BF16)
        send1[j, :, dim:] = router_part[j * FRESH : (j + 1) * FRESH].astype(BF16)

    @pl.loop(1, n)
    def _(i):
        j = lax.rem(k + i, n)
        peer_copy(send1.at[j], recv1.at[k], r1_send.at[j], r1_recv.at[k], j).start()

    recv1[k] = send1[k]

    @pl.loop(1, n_dp)
    def _(i):
        u = lax.rem(v + i, n_dp)
        peer_copy(cols.at[v], cols.at[v], c_send.at[u], c_recv.at[v], k, dp=u).start()

    own_in = xin[k].astype(F32)
    own_scaled, own_inv = normalize(own_in)

    @pl.loop(1, n)
    def _(i):
        j = lax.rem(k + i, n)
        peer_copy(send1.at[j], recv1.at[j], r1_send.at[j], r1_recv.at[j], j).wait()

    summed = recv1[0].astype(F32)
    for j in range(1, n):
        summed = summed + recv1[j].astype(F32)
    fresh_out = own_in + summed[:, :dim]
    router_pre = summed[:, dim:] + bias_row
    router_act, router_slope = gelu_both(router_pre)
    r_out = rout_ref[...]
    gate = jax.nn.sigmoid(jnp.sum(router_act * r_out, axis=1, keepdims=True))
    gap = live * (fresh_out - cached_rows)
    new_rows = (cached_rows + gate * gap).astype(BF16).astype(F32)
    gate_slope = gate * (1.0 - gate)
    hid_factor = gate_slope * r_out * router_slope
    out_factor = gate_slope * router_act

    def blend_out():
        turned = jnp.transpose(hot)
        kept = cached[...].astype(F32)
        mixed = jnp.where(
            turned[:, 0:1] > 0.5,
            new_rows[0:1],
            jnp.where(turned[:, 1:2] > 0.5, new_rows[1:2], kept),
        )
        blend[...] = mixed.astype(BF16)
        pltpu.make_async_copy(blend, blended_hbm, out_sem).start()

    slot = v * n + k
    delta_copy = peer_copy(delta, delta_in, aux_sems.at[0], aux_sems.at[1], k, pipe=1 - p)
    factor_copy = peer_copy(factors, factors_in, aux_sems.at[2], aux_sems.at[3], k, pipe=1 - p)

    @pl.when(is0)
    def _():
        moved = jnp.where(
            same_0 > 0.5, new_rows[0:1], jnp.where(same_1 > 0.5, new_rows[1:2], other_rows)
        )
        in1[...] = moved.astype(BF16)

        @pl.loop(0, n)
        def _(i):
            j = lax.rem(k + i, n)
            peer_copy(in1, xin.at[k], f_send.at[j], x_recv.at[k], j, pipe=1).start()

        delta[...] = gap
        factors[0:FRESH, :] = hid_factor
        factors[FRESH : 2 * FRESH, :] = out_factor
        delta_copy.start()
        factor_copy.start()
        blend_out()

        @pl.loop(0, n)
        def _(j):
            peer_copy(in1, xin.at[j], f_send.at[j], x_recv.at[j], j, pipe=1).wait_send()

        delta_copy.wait_send()
        factor_copy.wait_send()

        @pl.loop(0, n * n_dp)
        def _(j):
            peer_copy(
                gmsg.at[j], gmsg.at[j], g_send.at[j], g_recv.at[j], k, pipe=1
            ).wait_recv()

    def message(ref, gate_grad, hid_fac, out_fac):
        ref[0:FRESH, :] = gate_grad * hid_fac
        ref[FRESH : FRESH + 1, :] = jnp.sum(gate_grad * out_fac, axis=0, keepdims=True)
        ref[FRESH + 1 : FRESH + 2, :] = step_val.astype(F32)

    @pl.when(is1)
    def _():
        gate_grad = jnp.sum(picked * gap, axis=1, keepdims=True)
        fresh_grad = picked * (live * gate)
        fgrad[k] = fresh_grad.astype(BF16)

        @pl.loop(1, n)
        def _(i):
            j = lax.rem(k + i, n)
            peer_copy(fgrad.at[k], fgrad.at[k], f_send.at[j], f_recv.at[k], j).start()

        message(gmsg.at[slot], gate_grad, hid_factor, out_factor)

        @pl.loop(1, n * n_dp)
        def _(i):
            t = lax.rem(slot + i, n * n_dp)
            peer_copy(
                gmsg.at[slot], gmsg.at[slot], g_send.at[t], g_recv.at[slot], lax.rem(t, n), dp=t // n
            ).start()

        blend_out()

        @pl.loop(1, n)
        def _(i):
            j = lax.rem(k + i, n)
            peer_copy(fgrad.at[j], fgrad.at[j], f_send.at[j], f_recv.at[j], j).wait()

        for j in range(n):
            x32[j * FRESH : (j + 1) * FRESH, :] = fgrad[j].astype(F32)
        act_grad = dot_nt(x32[...].astype(BF16), down[...])
        pre_grad = (act_grad * pre[...]).astype(BF16)
        total[...] = dot_nn(pre_grad, up[...])

        @pl.loop(1, n * n_dp)
        def _(i):
            t = lax.rem(slot + i, n * n_dp)
            peer_copy(
                gmsg.at[t], gmsg.at[t], g_send.at[t], g_recv.at[t], lax.rem(t, n), dp=t // n
            ).wait()

        for j in range(n):
            hid[j * FRESH : (j + 1) * FRESH, :] = gmsg[v * n + j, 0:FRESH, :]
        router_term = dot_nt(hid[0:rows, :].astype(BF16), rin_ref[...])
        for j in range(n):

            @pl.when(k == j)
            def _():
                total[:, j * cols_n : (j + 1) * cols_n] += router_term

        grads = total[...]
        for j in range(n):
            send2[j] = grads[j * FRESH : (j + 1) * FRESH].astype(BF16)

        @pl.loop(1, n)
        def _(i):
            j = lax.rem(k + i, n)
            peer_copy(send2.at[j], recv2.at[k], r2_send.at[j], r2_recv.at[k], j).start()

        recv2[k] = send2[k]
        delta_copy.wait_recv()
        factor_copy.wait_recv()

        @pl.loop(1, n)
        def _(i):
            j = lax.rem(k + i, n)
            peer_copy(send2.at[j], recv2.at[j], r2_send.at[j], r2_recv.at[j], j).wait()

        back = recv2[0].astype(F32)
        for j in range(1, n):
            back = back + recv2[j].astype(F32)
        input_grad = fresh_grad + normalize_back(own_scaled, own_inv, back)
        cot_first = same_0 * input_grad[0:1] + same_1 * input_grad[1:2]
        gate_grad_first = jnp.sum(cot_first * delta_in[...], axis=1, keepdims=True)
        message(
            gfirst,
            gate_grad_first,
            factors_in[0:FRESH, :],
            factors_in[FRESH : 2 * FRESH, :],
        )

        @pl.loop(0, n * n_dp)
        def _(i):
            t = lax.rem(slot + i, n * n_dp)
            peer_copy(
                gfirst, gmsg.at[slot], g_send.at[t], g_recv.at[slot], lax.rem(t, n), pipe=0, dp=t // n
            ).start()

    @pl.loop(1, n_dp)
    def _(i):
        u = lax.rem(v + i, n_dp)
        peer_copy(cols.at[u], cols.at[u], c_send.at[u], c_recv.at[u], k, dp=u).wait()

    bias_total = jnp.zeros(bias_grad_ref.shape, F32)
    out_total = jnp.zeros((1, rh), F32)
    step_all = step_row.astype(F32)
    for u in range(n_dp):
        summed_bias = jnp.zeros((1, rh), F32)
        for j in range(n):
            got = gmsg[u * n + j]
            hid[(u * n + j) * FRESH : (u * n + j + 1) * FRESH, :] = got[0:FRESH]
            summed_bias = summed_bias + jnp.sum(got[0:FRESH], axis=0, keepdims=True)
            out_total = out_total + got[FRESH : FRESH + 1]
        at = gmsg[u * n, FRESH + 1 : FRESH + 2, :]
        bias_total = bias_total + jnp.where(step_all == at, summed_bias, 0.0)
    bias_grad_ref[...] = bias_total
    out_grad_ref[...] = out_total
    cols_all = cols[...].reshape(n_dp * rows, cols_n)
    in_grad_ref[...] = dot_tn(cols_all, hid[...].astype(BF16))

    @pl.when(is1)
    def _():
        @pl.loop(0, n * n_dp)
        def _(t):
            peer_copy(
                gfirst, gmsg.at[t], g_send.at[t], g_recv.at[t], lax.rem(t, n), pipe=0, dp=t // n
            ).wait_send()

    pltpu.make_async_copy(blend, blended_hbm, out_sem).wait()


def body(
    n,
    n_dp,
    video_tokens,
    cached_out,
    fresh_mask,
    timestep,
    up_weight,
    down_weight,
    router_in,
    router_bias,
    router_out,
    out_cotangent,
):
    toks, dim = video_tokens.shape[1:]
    hidden = up_weight.shape[1]
    cols_n, rh = router_in.shape[1:]
    steps = router_bias.shape[1]
    rows = n * FRESH
    hbm = pl.BlockSpec(memory_space=pl.ANY)
    vmem = pl.BlockSpec(memory_space=pltpu.VMEM)
    smem = pl.BlockSpec(memory_space=pltpu.SMEM)
    dma = pltpu.SemaphoreType.DMA
    outs = pl.pallas_call(
        functools.partial(kernel, n, n_dp),
        out_shape=(
            jax.ShapeDtypeStruct((toks, dim), BF16),
            jax.ShapeDtypeStruct((cols_n, rh), F32),
            jax.ShapeDtypeStruct((steps, rh), F32),
            jax.ShapeDtypeStruct((1, rh), F32),
        ),
        in_specs=[hbm, hbm, vmem, smem, hbm, hbm, vmem, vmem, vmem, hbm],
        out_specs=(hbm, vmem, vmem, vmem),
        scratch_shapes=[
            pltpu.VMEM((hidden, dim), BF16),
            pltpu.VMEM((hidden, dim), BF16),
            pltpu.VMEM((toks, dim), BF16),
            pltpu.VMEM((toks, dim), BF16),
            pltpu.VMEM((toks, dim), BF16),
            pltpu.VMEM((8, toks), F32),
            pltpu.VMEM((8, toks), F32),
            pltpu.VMEM((n, FRESH, dim), BF16),
            pltpu.VMEM((FRESH, dim), BF16),
            pltpu.VMEM((rows, dim), F32),
            pltpu.VMEM((rows, hidden), F32),
            pltpu.VMEM((n, FRESH, dim + rh), BF16),
            pltpu.VMEM((n, FRESH, dim + rh), BF16),
            pltpu.VMEM((FRESH, dim), F32),
            pltpu.VMEM((FRESH, dim), F32),
            pltpu.VMEM((2 * FRESH, rh), F32),
            pltpu.VMEM((2 * FRESH, rh), F32),
            pltpu.VMEM((n, FRESH, dim), BF16),
            pltpu.VMEM((rows, dim), F32),
            pltpu.VMEM((n, FRESH, dim), BF16),
            pltpu.VMEM((n, FRESH, dim), BF16),
            pltpu.VMEM((n_dp, rows, cols_n), BF16),
            pltpu.VMEM((n * n_dp, FRESH + 2, rh), F32),
            pltpu.VMEM((FRESH + 2, rh), F32),
            pltpu.VMEM((n_dp * rows, rh), F32),
            dma((4,)),
            dma((2,)),
            dma((n,)),
            dma((n,)),
            dma((n,)),
            dma((n,)),
            dma((4,)),
            dma((n,)),
            dma((n,)),
            dma((n,)),
            dma((n,)),
            dma((n_dp,)),
            dma((n_dp,)),
            dma((n * n_dp,)),
            dma((n * n_dp,)),
            dma,
        ],
        compiler_params=pltpu.CompilerParams(
            collective_id=0, has_side_effects=True, vmem_limit_bytes=48 * 1024 * 1024
        ),
    )(
        video_tokens[0],
        cached_out[0, 0],
        fresh_mask[0],
        timestep,
        up_weight[0],
        down_weight[0],
        router_in[0],
        router_bias[0],
        router_out,
        out_cotangent[0],
    )
    blended, in_grad, bias_grad, out_grad = outs
    return (blended[None, None], in_grad[None], bias_grad[None], out_grad)


def solution(mesh):
    placed = (
        P("dp", "fsdp", None),
        P("pipe", "dp", "fsdp", None),
        P("pipe", "dp", "fsdp"),
        P("dp"),
        P("pipe", "fsdp", None),
        P("pipe", "fsdp", None),
        P("pipe", "fsdp", None),
        P("pipe", None, None),
        P("pipe", None),
        P("dp", "fsdp", None),
    )
    return jax.shard_map(
        functools.partial(body, mesh.shape["fsdp"], mesh.shape["dp"]),
        mesh=mesh,
        in_specs=placed,
        out_specs=(
            P("pipe", "dp", "fsdp", None),
            P("pipe", "fsdp", None),
            P("pipe", None, None),
            P("pipe", None),
        ),
        check_vma=False,
    )
```

```python
import functools

import jax
import jax.numpy as jnp
from jax import lax
from jax.experimental import pallas as pl
from jax.experimental.pallas import tpu as pltpu
from jax.sharding import PartitionSpec as P

FRESH = 2

layer_eps = 1e-06
gelu_scale = 0.7978845608028654
gelu_cubic = 0.044715
F32 = jnp.float32
BF16 = jnp.bfloat16
MESH = pl.DeviceIdType.MESH


def gelu_both(values):
    inner_arg = gelu_scale * (values + gelu_cubic * values * values * values)
    tanh_val = jnp.tanh(inner_arg)
    gelu = 0.5 * values * (1.0 + tanh_val)
    slope = 0.5 * (1.0 + tanh_val) + 0.5 * values * (1.0 - tanh_val * tanh_val) * gelu_scale * (
        1.0 + 3.0 * gelu_cubic * values * values
    )
    return gelu, slope


def normalize(values):
    center = values - jnp.mean(values, axis=1, keepdims=True)
    inv_std = lax.rsqrt(jnp.mean(center * center, axis=1, keepdims=True) + layer_eps)
    return center * inv_std, inv_std


def normalize_back(scaled, inv_std, grads):
    return inv_std * (
        grads
        - jnp.mean(grads, axis=1, keepdims=True)
        - scaled * jnp.mean(grads * scaled, axis=1, keepdims=True)
    )


def dot_nn(left, right):
    return jnp.dot(left, right, preferred_element_type=F32)


def dot_nt(left, right):
    return lax.dot_general(left, right, (((1,), (1,)), ((), ())), preferred_element_type=F32)


def dot_tn(left, right):
    return lax.dot_general(left, right, (((0,), (0,)), ((), ())), preferred_element_type=F32)


def kernel(
    n,
    n_dp,
    tokens_hbm,
    cached_hbm,
    mask_hbm,
    step_ref,
    up_hbm,
    down_hbm,
    rin_hbm,
    bias_hbm,
    rout_hbm,
    cot_hbm,
    blended_hbm,
    in_grad_hbm,
    bias_grad_hbm,
    out_grad_hbm,
    up,
    down,
    first,
    cached,
    blend,
    mask_ref,
    rin_ref,
    bias_ref,
    rout_ref,
    in_grad_ref,
    bias_grad_ref,
    out_grad_ref,
    sel,
    psel,
    xin,
    win,
    cin,
    in1,
    w1,
    x32,
    c32,
    part_s,
    slope_ref,
    act_grad,
    send1,
    recv1,
    send2,
    recv2,
    delta,
    delta_in,
    factors,
    factors_in,
    cols,
    gmsg,
    gfirst,
    hid,
    load_sem,
    sel_sems,
    x_send,
    x_recv,
    w_send,
    w_recv,
    r1_send,
    r1_recv,
    r2_send,
    r2_recv,
    aux_sems,
    f_send,
    c_send,
    c_recv,
    g_send,
    g_recv,
    out_sem,
):
    k = lax.axis_index("fsdp")
    p = lax.axis_index("pipe")
    v = lax.axis_index("dp")
    is0 = p == 0
    is1 = p == 1
    dim = up.shape[1]
    rh = rin_ref.shape[1]
    cols_n = rin_ref.shape[0]
    rows = n * FRESH

    load_mask = pltpu.make_async_copy(mask_hbm, mask_ref, load_sem.at[0])
    load_rows = pltpu.make_async_copy(tokens_hbm, first, load_sem.at[1])
    load_cot = pltpu.make_async_copy(cot_hbm, first, load_sem.at[1])
    later = [
        pltpu.make_async_copy(cached_hbm, cached, load_sem.at[2]),
        pltpu.make_async_copy(up_hbm, up, load_sem.at[3]),
        pltpu.make_async_copy(down_hbm, down, load_sem.at[4]),
        pltpu.make_async_copy(rin_hbm, rin_ref, load_sem.at[5]),
        pltpu.make_async_copy(bias_hbm, bias_ref, load_sem.at[6]),
        pltpu.make_async_copy(rout_hbm, rout_ref, load_sem.at[7]),
    ]
    load_mask.start()

    @pl.when(is0)
    def _():
        load_rows.start()

    @pl.when(is1)
    def _():
        load_cot.start()

    barrier = pltpu.get_barrier_semaphore()
    count = n * 2 * n_dp
    flat = (k * 2 + p) * n_dp + v

    @pl.loop(1, count)
    def _(i):
        other = lax.rem(flat + i, count)
        pl.semaphore_signal(
            barrier,
            inc=1,
            device_id={
                "fsdp": other // (2 * n_dp),
                "pipe": lax.rem(other // n_dp, 2),
                "dp": lax.rem(other, n_dp),
            },
            device_id_type=MESH,
        )

    for load in later:
        load.start()

    load_mask.wait()
    toks = mask_ref.shape[1]
    lane = lax.broadcasted_iota(jnp.int32, (1, toks), 1).astype(F32)
    fresh = mask_ref[...] > 0
    low = jnp.min(jnp.where(fresh, lane, float(toks)), axis=1, keepdims=True)
    high = jnp.max(jnp.where(fresh, lane, -1.0), axis=1, keepdims=True)
    hot_low = jnp.where(lane == low, 1.0, 0.0)
    hot_high = jnp.where(jnp.logical_and(lane == high, high > low), 1.0, 0.0)
    row8 = lax.broadcasted_iota(jnp.int32, (8, toks), 0)
    hot = jnp.where(row8 == 0, hot_low, jnp.where(row8 == 1, hot_high, 0.0))
    sel[...] = hot
    hot_b = hot.astype(BF16)
    live = jnp.sum(hot, axis=1, keepdims=True)[:FRESH]

    load_rows.wait()
    picked = dot_nn(hot_b, first[...])[:FRESH]

    @pl.when(is0)
    def _():
        xin[k] = picked.astype(BF16)

    @pl.when(is1)
    def _():
        cin[k] = picked.astype(BF16)

    pl.semaphore_wait(barrier, count - 1)

    def peer_copy(src, dst, send_sem, recv_sem, j, **where):
        return pltpu.make_async_remote_copy(
            src_ref=src,
            dst_ref=dst,
            send_sem=send_sem,
            recv_sem=recv_sem,
            device_id={"fsdp": j, "pipe": p, "dp": v, **where},
            device_id_type=MESH,
        )

    @pl.when(is0)
    def _():
        @pl.loop(1, n)
        def _(i):
            j = lax.rem(k + i, n)
            peer_copy(xin.at[k], xin.at[k], x_send.at[j], x_recv.at[k], j).start()

    @pl.when(is1)
    def _():
        @pl.loop(1, n)
        def _(i):
            j = lax.rem(k + i, n)
            peer_copy(cin.at[k], cin.at[k], x_send.at[j], c_recv.at[k], j).start()

    sel_copy = peer_copy(sel, psel, sel_sems.at[0], sel_sems.at[1], k, pipe=1 - p)
    sel_copy.start()
    for load in later:
        load.wait()
    cached_rows = dot_nn(hot_b, cached[...])[:FRESH]
    sel_copy.wait()
    other_hot = psel[...]
    same_0 = jnp.sum(other_hot[:FRESH] * hot[0:1], axis=1, keepdims=True)
    same_1 = jnp.sum(other_hot[:FRESH] * hot[1:2], axis=1, keepdims=True)
    other_rows = dot_nn(other_hot.astype(BF16), cached[...])[:FRESH]
    step_val = jnp.full((1, rh), step_ref[0], jnp.int32)
    bias_row = bias_ref[step_ref[0]]
    r_out = rout_ref[...]

    @pl.when(is0)
    def _():
        @pl.loop(1, n)
        def _(i):
            j = lax.rem(k + i, n)
            peer_copy(xin.at[j], xin.at[j], x_send.at[j], x_recv.at[j], j).wait()

    @pl.when(is1)
    def _():
        @pl.loop(1, n)
        def _(i):
            j = lax.rem(k + i, n)
            peer_copy(cin.at[j], cin.at[j], x_send.at[j], c_recv.at[j], j).wait()

        for j in range(n):
            c32[j * FRESH : (j + 1) * FRESH, :] = cin[j].astype(F32)
        act_grad[...] = dot_nt(c32[...].astype(BF16), down[...])

        @pl.loop(0, n)
        def _(j):
            peer_copy(xin.at[j], xin.at[j], x_send.at[j], x_recv.at[j], j, pipe=0).wait_recv()

    for j in range(n):
        x32[j * FRESH : (j + 1) * FRESH, :] = xin[j].astype(F32)
    scaled_all, _ = normalize(x32[...])
    x32[...] = scaled_all
    normed = scaled_all.astype(BF16)
    for j in range(n):

        @pl.when(k == j)
        def _():
            cols[v] = x32[:, j * cols_n : (j + 1) * cols_n].astype(BF16)

    router_part = dot_nn(cols[v], rin_ref[...])
    pre_act = dot_nt(normed, up[...])
    act, slope = gelu_both(pre_act)
    slope_ref[...] = slope
    term = dot_nn(act.astype(BF16), down[...])
    for j in range(n):
        send1[j, :, :dim] = term[j * FRESH : (j + 1) * FRESH].astype(BF16)
        send1[j, :, dim:] = router_part[j * FRESH : (j + 1) * FRESH].astype(BF16)

    @pl.loop(1, n)
    def _(i):
        j = lax.rem(k + i, n)
        peer_copy(send1.at[j], recv1.at[k], r1_send.at[j], r1_recv.at[k], j).start()

    @pl.when(is1)
    def _():
        @pl.loop(0, n)
        def _(j):
            peer_copy(win.at[j], win.at[j], x_send.at[j], w_recv.at[j], j, pipe=0).wait_recv()

        for j in range(n):
            c32[j * FRESH : (j + 1) * FRESH, :] = win[j].astype(F32)
        for j in range(n):

            @pl.when(k == j)
            def _():
                part_s[:, 0:rh] = dot_nn(
                    c32[:, j * cols_n : (j + 1) * cols_n].astype(BF16), rin_ref[...]
                )

        up_w = dot_nt(c32[...].astype(BF16), up[...])
        along = jnp.sum(act_grad[...] * slope_ref[...] * up_w, axis=1, keepdims=True)
        part_s[:, rh:] = jnp.broadcast_to(along, (rows, part_s.shape[1] - rh))
        for j in range(n):
            send2[j] = part_s[j * FRESH : (j + 1) * FRESH, :]

        @pl.loop(1, n)
        def _(i):
            j = lax.rem(k + i, n)
            peer_copy(send2.at[j], recv2.at[k], r2_send.at[j], r2_recv.at[k], j).start()

        recv2[k] = send2[k]

    recv1[k] = send1[k]

    @pl.loop(1, n_dp)
    def _(i):
        u = lax.rem(v + i, n_dp)
        peer_copy(cols.at[v], cols.at[v], c_send.at[u], g_recv.at[n * n_dp + v], k, dp=u).start()

    own_in = xin[k].astype(F32)

    @pl.loop(1, n)
    def _(i):
        j = lax.rem(k + i, n)
        peer_copy(send1.at[j], recv1.at[j], r1_send.at[j], r1_recv.at[j], j).wait()

    summed = recv1[0].astype(F32)
    for j in range(1, n):
        summed = summed + recv1[j].astype(F32)
    fresh_out = own_in + summed[:, :dim]
    router_pre = summed[:, dim:] + bias_row
    router_act, router_slope = gelu_both(router_pre)
    gate = jax.nn.sigmoid(jnp.sum(router_act * r_out, axis=1, keepdims=True))
    gap = live * (fresh_out - cached_rows)
    new_rows = (cached_rows + gate * gap).astype(BF16).astype(F32)
    gate_slope = gate * (1.0 - gate)
    hid_factor = gate_slope * r_out * router_slope
    out_factor = gate_slope * router_act

    def blend_out():
        turned = jnp.transpose(hot)
        kept = cached[...].astype(F32)
        mixed = jnp.where(
            turned[:, 0:1] > 0.5,
            new_rows[0:1],
            jnp.where(turned[:, 1:2] > 0.5, new_rows[1:2], kept),
        )
        blend[...] = mixed.astype(BF16)
        pltpu.make_async_copy(blend, blended_hbm, out_sem.at[0]).start()

    slot = v * n + k
    delta_copy = peer_copy(delta, delta_in, aux_sems.at[0], aux_sems.at[1], k, pipe=1 - p)
    factor_copy = peer_copy(factors, factors_in, aux_sems.at[2], aux_sems.at[3], k, pipe=1 - p)

    @pl.when(is0)
    def _():
        moved = jnp.where(
            same_0 > 0.5, new_rows[0:1], jnp.where(same_1 > 0.5, new_rows[1:2], other_rows)
        )
        in1[...] = moved.astype(BF16)

        @pl.loop(0, n)
        def _(i):
            j = lax.rem(k + i, n)
            peer_copy(in1, xin.at[k], f_send.at[j], x_recv.at[k], j, pipe=1).start()

        met = same_0 * gap[0:1] + same_1 * gap[1:2]
        scaled, inv_std = normalize(moved)
        w1[...] = normalize_back(scaled, inv_std, met).astype(BF16)

        @pl.loop(0, n)
        def _(i):
            j = lax.rem(k + i, n)
            peer_copy(w1, win.at[k], w_send.at[j], w_recv.at[k], j, pipe=1).start()

        delta[...] = met
        factors[0:FRESH, :] = hid_factor
        factors[FRESH : 2 * FRESH, :] = out_factor
        delta_copy.start()
        factor_copy.start()
        blend_out()

        @pl.loop(0, n)
        def _(j):
            peer_copy(in1, xin.at[j], f_send.at[j], x_recv.at[j], j, pipe=1).wait_send()
            peer_copy(w1, win.at[j], w_send.at[j], w_recv.at[j], j, pipe=1).wait_send()

        delta_copy.wait_send()
        factor_copy.wait_send()

        @pl.loop(0, n * n_dp)
        def _(j):
            peer_copy(
                gmsg.at[j], gmsg.at[j], g_send.at[j], g_recv.at[j], k, pipe=1
            ).wait_recv()

    def message(ref, gate_grad, hid_fac, out_fac):
        ref[0:FRESH, :] = gate_grad * hid_fac
        ref[FRESH : FRESH + 1, :] = jnp.sum(gate_grad * out_fac, axis=0, keepdims=True)
        ref[FRESH + 1 : FRESH + 2, :] = step_val.astype(F32)

    @pl.when(is1)
    def _():
        gate_grad = jnp.sum(picked * gap, axis=1, keepdims=True)
        message(gmsg.at[slot], gate_grad, hid_factor, out_factor)

        @pl.loop(1, n * n_dp)
        def _(i):
            t = lax.rem(slot + i, n * n_dp)
            peer_copy(
                gmsg.at[slot], gmsg.at[slot], g_send.at[t], g_recv.at[slot], lax.rem(t, n), dp=t // n
            ).start()

        delta_copy.wait_recv()
        factor_copy.wait_recv()
        straight = jnp.sum(picked * delta_in[...], axis=1, keepdims=True)

        @pl.loop(1, n)
        def _(i):
            j = lax.rem(k + i, n)
            peer_copy(send2.at[j], recv2.at[j], r2_send.at[j], r2_recv.at[j], j).wait()

        through = recv2[0]
        for j in range(1, n):
            through = through + recv2[j]
        met_grad = live * gate * (straight + through[:, rh : rh + 1]) + jnp.sum(
            gate_grad * hid_factor * through[:, 0:rh], axis=1, keepdims=True
        )
        gate_grad_first = same_0 * met_grad[0:1] + same_1 * met_grad[1:2]
        message(
            gfirst,
            gate_grad_first,
            factors_in[0:FRESH, :],
            factors_in[FRESH : 2 * FRESH, :],
        )

        @pl.loop(0, n * n_dp)
        def _(i):
            t = lax.rem(slot + i, n * n_dp)
            peer_copy(
                gfirst,
                gmsg.at[slot],
                g_send.at[n * n_dp + t],
                g_recv.at[slot],
                lax.rem(t, n),
                pipe=0,
                dp=t // n,
            ).start()

        blend_out()

        @pl.loop(1, n * n_dp)
        def _(i):
            t = lax.rem(slot + i, n * n_dp)
            peer_copy(
                gmsg.at[t], gmsg.at[t], g_send.at[t], g_recv.at[t], lax.rem(t, n), dp=t // n
            ).wait()

    @pl.loop(1, n_dp)
    def _(i):
        u = lax.rem(v + i, n_dp)
        peer_copy(cols.at[u], cols.at[u], c_send.at[u], g_recv.at[n * n_dp + u], k, dp=u).wait()

    out_total = jnp.zeros((1, rh), F32)
    bias_sums = []
    for u in range(n_dp):
        summed_bias = jnp.zeros((1, rh), F32)
        for j in range(n):
            got = gmsg[u * n + j]
            hid[(u * n + j) * FRESH : (u * n + j + 1) * FRESH, :] = got[0:FRESH]
            summed_bias = summed_bias + jnp.sum(got[0:FRESH], axis=0, keepdims=True)
            out_total = out_total + got[FRESH : FRESH + 1]
        bias_sums.append((gmsg[u * n, FRESH + 1 : FRESH + 2, :], summed_bias))
    cols_all = cols[...].reshape(n_dp * rows, cols_n)
    in_grad_ref[...] = dot_tn(cols_all, hid[...].astype(BF16))
    put_in = pltpu.make_async_copy(in_grad_ref, in_grad_hbm, out_sem.at[1])
    put_in.start()
    step_all = lax.broadcasted_iota(jnp.int32, bias_grad_ref.shape, 0).astype(F32)
    bias_total = jnp.zeros(bias_grad_ref.shape, F32)
    for at, summed_bias in bias_sums:
        bias_total = bias_total + jnp.where(step_all == at[None], summed_bias[None], 0.0)
    bias_grad_ref[...] = bias_total
    out_grad_ref[...] = out_total
    put_bias = pltpu.make_async_copy(bias_grad_ref, bias_grad_hbm, out_sem.at[2])
    put_out = pltpu.make_async_copy(out_grad_ref, out_grad_hbm, out_sem.at[3])
    put_bias.start()
    put_out.start()

    @pl.when(is1)
    def _():
        @pl.loop(0, n * n_dp)
        def _(t):
            peer_copy(
                gfirst,
                gmsg.at[t],
                g_send.at[n * n_dp + t],
                g_recv.at[t],
                lax.rem(t, n),
                pipe=0,
                dp=t // n,
            ).wait_send()

    pltpu.make_async_copy(blend, blended_hbm, out_sem.at[0]).wait()
    put_in.wait()
    put_bias.wait()
    put_out.wait()


def body(
    n,
    n_dp,
    video_tokens,
    cached_out,
    fresh_mask,
    timestep,
    up_weight,
    down_weight,
    router_in,
    router_bias,
    router_out,
    out_cotangent,
):
    toks, dim = video_tokens.shape[1:]
    hidden = up_weight.shape[1]
    cols_n, rh = router_in.shape[1:]
    steps = router_bias.shape[1]
    rows = n * FRESH
    hbm = pl.BlockSpec(memory_space=pl.ANY)
    smem = pl.BlockSpec(memory_space=pltpu.SMEM)
    dma = pltpu.SemaphoreType.DMA
    outs = pl.pallas_call(
        functools.partial(kernel, n, n_dp),
        out_shape=(
            jax.ShapeDtypeStruct((toks, dim), BF16),
            jax.ShapeDtypeStruct((cols_n, rh), F32),
            jax.ShapeDtypeStruct((steps, 1, rh), F32),
            jax.ShapeDtypeStruct((1, rh), F32),
        ),
        in_specs=[hbm, hbm, hbm, smem] + [hbm] * 6,
        out_specs=(hbm,) * 4,
        scratch_shapes=[
            pltpu.VMEM((hidden, dim), BF16),
            pltpu.VMEM((hidden, dim), BF16),
            pltpu.VMEM((toks, dim), BF16),
            pltpu.VMEM((toks, dim), BF16),
            pltpu.VMEM((toks, dim), BF16),
            pltpu.VMEM((1, toks), jnp.int32),
            pltpu.VMEM((cols_n, rh), BF16),
            pltpu.VMEM((steps, 1, rh), F32),
            pltpu.VMEM((1, rh), F32),
            pltpu.VMEM((cols_n, rh), F32),
            pltpu.VMEM((steps, 1, rh), F32),
            pltpu.VMEM((1, rh), F32),
            pltpu.VMEM((8, toks), F32),
            pltpu.VMEM((8, toks), F32),
            pltpu.VMEM((n, FRESH, dim), BF16),
            pltpu.VMEM((n, FRESH, dim), BF16),
            pltpu.VMEM((n, FRESH, dim), BF16),
            pltpu.VMEM((FRESH, dim), BF16),
            pltpu.VMEM((FRESH, dim), BF16),
            pltpu.VMEM((rows, dim), F32),
            pltpu.VMEM((rows, dim), F32),
            pltpu.VMEM((rows, rh + 128), F32),
            pltpu.VMEM((rows, hidden), F32),
            pltpu.VMEM((rows, hidden), F32),
            pltpu.VMEM((n, FRESH, dim + rh), BF16),
            pltpu.VMEM((n, FRESH, dim + rh), BF16),
            pltpu.VMEM((n, FRESH, rh + 128), F32),
            pltpu.VMEM((n, FRESH, rh + 128), F32),
            pltpu.VMEM((FRESH, dim), F32),
            pltpu.VMEM((FRESH, dim), F32),
            pltpu.VMEM((2 * FRESH, rh), F32),
            pltpu.VMEM((2 * FRESH, rh), F32),
            pltpu.VMEM((n_dp, rows, cols_n), BF16),
            pltpu.VMEM((n * n_dp, FRESH + 2, rh), F32),
            pltpu.VMEM((FRESH + 2, rh), F32),
            pltpu.VMEM((n_dp * rows, rh), F32),
            dma((8,)),
            dma((2,)),
            dma((n,)),
            dma((n,)),
            dma((n,)),
            dma((n,)),
            dma((n,)),
            dma((n,)),
            dma((n,)),
            dma((n,)),
            dma((4,)),
            dma((n,)),
            dma((n_dp,)),
            dma((n,)),
            dma((2 * n * n_dp,)),
            dma((n * n_dp + n_dp,)),
            dma((4,)),
        ],
        compiler_params=pltpu.CompilerParams(
            collective_id=0, has_side_effects=True, vmem_limit_bytes=67043328
        ),
    )(
        video_tokens[0],
        cached_out[0, 0],
        fresh_mask[0],
        timestep,
        up_weight[0],
        down_weight[0],
        router_in[0],
        jnp.transpose(router_bias, (1, 0, 2)),
        router_out,
        out_cotangent[0],
    )
    blended, in_grad, bias_grad, out_grad = outs
    return (blended[None, None], in_grad[None], jnp.transpose(bias_grad, (1, 0, 2)), out_grad)


def solution(mesh):
    placed = (
        P("dp", "fsdp", None),
        P("pipe", "dp", "fsdp", None),
        P("pipe", "dp", "fsdp"),
        P("dp"),
        P("pipe", "fsdp", None),
        P("pipe", "fsdp", None),
        P("pipe", "fsdp", None),
        P("pipe", None, None),
        P("pipe", None),
        P("dp", "fsdp", None),
    )
    return jax.shard_map(
        functools.partial(body, mesh.shape["fsdp"], mesh.shape["dp"]),
        mesh=mesh,
        in_specs=placed,
        out_specs=(
            P("pipe", "dp", "fsdp", None),
            P("pipe", "fsdp", None),
            P("pipe", None, None),
            P("pipe", None),
        ),
        check_vma=False,
    )
```

```python
import functools

import jax
import jax.numpy as jnp
from jax import lax
from jax.experimental import pallas as pl
from jax.experimental.pallas import tpu as pltpu
from jax.sharding import PartitionSpec as P

FRESH = 2

layer_eps = 1e-06
gelu_scale = 0.7978845608028654
gelu_cubic = 0.044715
F32 = jnp.float32
BF16 = jnp.bfloat16
MESH = pl.DeviceIdType.MESH


def gelu_both(values):
    inner_arg = gelu_scale * (values + gelu_cubic * values * values * values)
    tanh_val = jnp.tanh(inner_arg)
    gelu = 0.5 * values * (1.0 + tanh_val)
    slope = 0.5 * (1.0 + tanh_val) + 0.5 * values * (1.0 - tanh_val * tanh_val) * gelu_scale * (
        1.0 + 3.0 * gelu_cubic * values * values
    )
    return gelu, slope


def normalize(values):
    center = values - jnp.mean(values, axis=1, keepdims=True)
    inv_std = lax.rsqrt(jnp.mean(center * center, axis=1, keepdims=True) + layer_eps)
    return center * inv_std, inv_std


def normalize_back(scaled, inv_std, grads):
    return inv_std * (
        grads
        - jnp.mean(grads, axis=1, keepdims=True)
        - scaled * jnp.mean(grads * scaled, axis=1, keepdims=True)
    )


def dot_nn(left, right):
    return jnp.dot(left, right, preferred_element_type=F32)


def dot_nt(left, right):
    return lax.dot_general(left, right, (((1,), (1,)), ((), ())), preferred_element_type=F32)


def dot_tn(left, right):
    return lax.dot_general(left, right, (((0,), (0,)), ((), ())), preferred_element_type=F32)


def kernel(
    n,
    n_dp,
    tokens_hbm,
    cached_hbm,
    mask_hbm,
    step_ref,
    up_hbm,
    down_hbm,
    rin_hbm,
    bias_hbm,
    rout_hbm,
    cot_hbm,
    blended_hbm,
    in_grad_hbm,
    bias_grad_hbm,
    out_grad_hbm,
    up,
    down,
    first,
    cached,
    blend,
    mask_ref,
    rin_ref,
    bias_ref,
    rout_ref,
    in_grad_ref,
    bias_grad_ref,
    out_grad_ref,
    sel,
    psel,
    xin,
    win,
    cin,
    in1,
    w1,
    x32,
    c32,
    part_s,
    slope_ref,
    act_grad,
    send1,
    recv1,
    send2,
    recv2,
    delta,
    delta_in,
    factors,
    factors_in,
    cols,
    gmsg,
    gfirst,
    hid,
    load_sem,
    sel_sems,
    x_send,
    x_recv,
    w_send,
    w_recv,
    r1_send,
    r1_recv,
    r2_send,
    r2_recv,
    aux_sems,
    f_send,
    c_send,
    c_recv,
    g_send,
    g_recv,
    out_sem,
):
    k = lax.axis_index("fsdp")
    p = lax.axis_index("pipe")
    v = lax.axis_index("dp")
    is0 = p == 0
    is1 = p == 1
    dim = up.shape[1]
    rh = rin_ref.shape[1]
    cols_n = rin_ref.shape[0]
    rows = n * FRESH

    load_mask = pltpu.make_async_copy(mask_hbm, mask_ref, load_sem.at[0])
    load_rows = pltpu.make_async_copy(tokens_hbm, first, load_sem.at[1])
    load_cot = pltpu.make_async_copy(cot_hbm, first, load_sem.at[1])
    later = [
        pltpu.make_async_copy(cached_hbm, cached, load_sem.at[2]),
        pltpu.make_async_copy(up_hbm, up, load_sem.at[3]),
        pltpu.make_async_copy(down_hbm, down, load_sem.at[4]),
        pltpu.make_async_copy(rin_hbm, rin_ref, load_sem.at[5]),
        pltpu.make_async_copy(bias_hbm, bias_ref, load_sem.at[6]),
        pltpu.make_async_copy(rout_hbm, rout_ref, load_sem.at[7]),
    ]
    load_mask.start()

    @pl.when(is0)
    def _():
        load_rows.start()

    @pl.when(is1)
    def _():
        load_cot.start()

    barrier = pltpu.get_barrier_semaphore()
    count = n * 2 * n_dp
    flat = (k * 2 + p) * n_dp + v

    @pl.loop(1, count)
    def _(i):
        other = lax.rem(flat + i, count)
        pl.semaphore_signal(
            barrier,
            inc=1,
            device_id={
                "fsdp": other // (2 * n_dp),
                "pipe": lax.rem(other // n_dp, 2),
                "dp": lax.rem(other, n_dp),
            },
            device_id_type=MESH,
        )

    for load in later:
        load.start()

    load_mask.wait()
    toks = mask_ref.shape[1]
    lane = lax.broadcasted_iota(jnp.int32, (1, toks), 1).astype(F32)
    fresh = mask_ref[...] > 0
    low = jnp.min(jnp.where(fresh, lane, float(toks)), axis=1, keepdims=True)
    high = jnp.max(jnp.where(fresh, lane, -1.0), axis=1, keepdims=True)
    hot_low = jnp.where(lane == low, 1.0, 0.0)
    hot_high = jnp.where(jnp.logical_and(lane == high, high > low), 1.0, 0.0)
    row8 = lax.broadcasted_iota(jnp.int32, (8, toks), 0)
    hot = jnp.where(row8 == 0, hot_low, jnp.where(row8 == 1, hot_high, 0.0))
    sel[...] = hot
    hot_b = hot.astype(BF16)
    live = jnp.sum(hot, axis=1, keepdims=True)[:FRESH]

    load_rows.wait()
    picked = dot_nn(hot_b, first[...])[:FRESH]

    @pl.when(is0)
    def _():
        xin[k] = picked.astype(BF16)

    @pl.when(is1)
    def _():
        cin[k] = picked.astype(BF16)

    pl.semaphore_wait(barrier, count - 1)

    def peer_copy(src, dst, send_sem, recv_sem, j, **where):
        return pltpu.make_async_remote_copy(
            src_ref=src,
            dst_ref=dst,
            send_sem=send_sem,
            recv_sem=recv_sem,
            device_id={"fsdp": j, "pipe": p, "dp": v, **where},
            device_id_type=MESH,
        )

    @pl.when(is0)
    def _():
        @pl.loop(1, n)
        def _(i):
            j = lax.rem(k + i, n)
            peer_copy(xin.at[k], xin.at[k], x_send.at[j], x_recv.at[k], j).start()

    @pl.when(is1)
    def _():
        @pl.loop(1, n)
        def _(i):
            j = lax.rem(k + i, n)
            peer_copy(cin.at[k], cin.at[k], x_send.at[j], c_recv.at[k], j).start()

    sel_copy = peer_copy(sel, psel, sel_sems.at[0], sel_sems.at[1], k, pipe=1 - p)
    sel_copy.start()
    for load in later:
        load.wait()
    cached_rows = dot_nn(hot_b, cached[...])[:FRESH]
    sel_copy.wait()
    other_hot = psel[...]
    same_0 = jnp.sum(other_hot[:FRESH] * hot[0:1], axis=1, keepdims=True)
    same_1 = jnp.sum(other_hot[:FRESH] * hot[1:2], axis=1, keepdims=True)
    other_rows = dot_nn(other_hot.astype(BF16), cached[...])[:FRESH]
    step_val = jnp.full((1, rh), step_ref[0], jnp.int32)
    bias_row = bias_ref[step_ref[0]]
    r_out = rout_ref[...]

    @pl.when(is0)
    def _():
        @pl.loop(1, n)
        def _(i):
            j = lax.rem(k + i, n)
            peer_copy(xin.at[j], xin.at[j], x_send.at[j], x_recv.at[j], j).wait()

    @pl.when(is1)
    def _():
        @pl.loop(1, n)
        def _(i):
            j = lax.rem(k + i, n)
            peer_copy(cin.at[j], cin.at[j], x_send.at[j], c_recv.at[j], j).wait()

        for j in range(n):
            c32[j * FRESH : (j + 1) * FRESH, :] = cin[j].astype(F32)
        act_grad[...] = dot_nt(c32[...].astype(BF16), down[...])

        @pl.loop(0, n)
        def _(j):
            peer_copy(xin.at[j], xin.at[j], x_send.at[j], x_recv.at[j], j, pipe=0).wait_recv()

    for j in range(n):
        x32[j * FRESH : (j + 1) * FRESH, :] = xin[j].astype(F32)
    scaled_all, _ = normalize(x32[...])
    x32[...] = scaled_all
    normed = scaled_all.astype(BF16)
    for j in range(n):

        @pl.when(k == j)
        def _():
            cols[v] = x32[:, j * cols_n : (j + 1) * cols_n].astype(BF16)

    router_part = dot_nn(cols[v], rin_ref[...])
    pre_act = dot_nt(normed, up[...])
    act, slope = gelu_both(pre_act)
    slope_ref[...] = slope
    term = dot_nn(act.astype(BF16), down[...])
    for j in range(n):
        send1[j, :, :dim] = term[j * FRESH : (j + 1) * FRESH].astype(BF16)
        send1[j, :, dim:] = router_part[j * FRESH : (j + 1) * FRESH].astype(BF16)

    @pl.loop(1, n)
    def _(i):
        j = lax.rem(k + i, n)
        peer_copy(send1.at[j], recv1.at[k], r1_send.at[j], r1_recv.at[k], j).start()

    @pl.when(is1)
    def _():
        @pl.loop(0, n)
        def _(j):
            peer_copy(win.at[j], win.at[j], x_send.at[j], w_recv.at[j], j, pipe=0).wait_recv()

        for j in range(n):
            c32[j * FRESH : (j + 1) * FRESH, :] = win[j].astype(F32)
        for j in range(n):

            @pl.when(k == j)
            def _():
                part_s[:, 0:rh] = dot_nn(
                    c32[:, j * cols_n : (j + 1) * cols_n].astype(BF16), rin_ref[...]
                )

        up_w = dot_nt(c32[...].astype(BF16), up[...])
        along = jnp.sum(act_grad[...] * slope_ref[...] * up_w, axis=1, keepdims=True)
        part_s[:, rh:] = jnp.broadcast_to(along, (rows, part_s.shape[1] - rh))
        for j in range(n):
            send2[j] = part_s[j * FRESH : (j + 1) * FRESH, :]

        @pl.loop(1, n)
        def _(i):
            j = lax.rem(k + i, n)
            peer_copy(send2.at[j], recv2.at[k], r2_send.at[j], r2_recv.at[k], j).start()

        recv2[k] = send2[k]

    recv1[k] = send1[k]

    @pl.loop(1, n_dp)
    def _(i):
        u = lax.rem(v + i, n_dp)
        peer_copy(cols.at[v], cols.at[v], c_send.at[u], g_recv.at[n * n_dp + v], k, dp=u).start()

    own_in = xin[k].astype(F32)

    @pl.loop(1, n)
    def _(i):
        j = lax.rem(k + i, n)
        peer_copy(send1.at[j], recv1.at[j], r1_send.at[j], r1_recv.at[j], j).wait()

    summed = recv1[0].astype(F32)
    for j in range(1, n):
        summed = summed + recv1[j].astype(F32)
    fresh_out = own_in + summed[:, :dim]
    router_pre = summed[:, dim:] + bias_row
    router_act, router_slope = gelu_both(router_pre)
    gate = jax.nn.sigmoid(jnp.sum(router_act * r_out, axis=1, keepdims=True))
    gap = live * (fresh_out - cached_rows)
    new_rows = (cached_rows + gate * gap).astype(BF16).astype(F32)
    gate_slope = gate * (1.0 - gate)
    hid_factor = gate_slope * r_out * router_slope
    out_factor = gate_slope * router_act

    def blend_out():
        turned = jnp.transpose(hot)
        kept = cached[...].astype(F32)
        mixed = jnp.where(
            turned[:, 0:1] > 0.5,
            new_rows[0:1],
            jnp.where(turned[:, 1:2] > 0.5, new_rows[1:2], kept),
        )
        blend[...] = mixed.astype(BF16)
        pltpu.make_async_copy(blend, blended_hbm, out_sem.at[0]).start()

    slot = v * n + k
    delta_copy = peer_copy(delta, delta_in, aux_sems.at[0], aux_sems.at[1], k, pipe=1 - p)
    factor_copy = peer_copy(factors, factors_in, aux_sems.at[2], aux_sems.at[3], k, pipe=1 - p)

    @pl.when(is0)
    def _():
        moved = jnp.where(
            same_0 > 0.5, new_rows[0:1], jnp.where(same_1 > 0.5, new_rows[1:2], other_rows)
        )
        in1[...] = moved.astype(BF16)

        @pl.loop(0, n)
        def _(i):
            j = lax.rem(k + i, n)
            peer_copy(in1, xin.at[k], f_send.at[j], x_recv.at[k], j, pipe=1).start()

        met = same_0 * gap[0:1] + same_1 * gap[1:2]
        scaled, inv_std = normalize(moved)
        w1[...] = normalize_back(scaled, inv_std, met).astype(BF16)

        @pl.loop(0, n)
        def _(i):
            j = lax.rem(k + i, n)
            peer_copy(w1, win.at[k], w_send.at[j], w_recv.at[k], j, pipe=1).start()

        delta[...] = met
        factors[0:FRESH, :] = hid_factor
        factors[FRESH : 2 * FRESH, :] = out_factor
        delta_copy.start()
        factor_copy.start()
        blend_out()

        @pl.loop(0, n)
        def _(j):
            peer_copy(in1, xin.at[j], f_send.at[j], x_recv.at[j], j, pipe=1).wait_send()
            peer_copy(w1, win.at[j], w_send.at[j], w_recv.at[j], j, pipe=1).wait_send()

        delta_copy.wait_send()
        factor_copy.wait_send()

        @pl.loop(0, n * n_dp)
        def _(j):
            peer_copy(
                gmsg.at[j], gmsg.at[j], g_send.at[j], g_recv.at[j], k, pipe=1
            ).wait_recv()

    def message(ref, gate_grad, hid_fac, out_fac):
        ref[0:FRESH, :] = gate_grad * hid_fac
        ref[FRESH : FRESH + 1, :] = jnp.sum(gate_grad * out_fac, axis=0, keepdims=True)
        ref[FRESH + 1 : FRESH + 2, :] = step_val.astype(F32)

    @pl.when(is1)
    def _():
        gate_grad = jnp.sum(picked * gap, axis=1, keepdims=True)
        message(gmsg.at[slot], gate_grad, hid_factor, out_factor)

        @pl.loop(1, n * n_dp)
        def _(i):
            t = lax.rem(slot + i, n * n_dp)
            peer_copy(
                gmsg.at[slot], gmsg.at[slot], g_send.at[t], g_recv.at[slot], lax.rem(t, n), dp=t // n
            ).start()

        delta_copy.wait_recv()
        factor_copy.wait_recv()
        straight = jnp.sum(picked * delta_in[...], axis=1, keepdims=True)

        @pl.loop(1, n)
        def _(i):
            j = lax.rem(k + i, n)
            peer_copy(send2.at[j], recv2.at[j], r2_send.at[j], r2_recv.at[j], j).wait()

        through = recv2[0]
        for j in range(1, n):
            through = through + recv2[j]
        met_grad = live * gate * (straight + through[:, rh : rh + 1]) + jnp.sum(
            gate_grad * hid_factor * through[:, 0:rh], axis=1, keepdims=True
        )
        gate_grad_first = same_0 * met_grad[0:1] + same_1 * met_grad[1:2]
        message(
            gfirst,
            gate_grad_first,
            factors_in[0:FRESH, :],
            factors_in[FRESH : 2 * FRESH, :],
        )

        @pl.loop(0, n * n_dp)
        def _(i):
            t = lax.rem(slot + i, n * n_dp)
            peer_copy(
                gfirst,
                gmsg.at[slot],
                g_send.at[n * n_dp + t],
                g_recv.at[slot],
                lax.rem(t, n),
                pipe=0,
                dp=t // n,
            ).start()

        blend_out()

        @pl.loop(1, n * n_dp)
        def _(i):
            t = lax.rem(slot + i, n * n_dp)
            peer_copy(
                gmsg.at[t], gmsg.at[t], g_send.at[t], g_recv.at[t], lax.rem(t, n), dp=t // n
            ).wait()

    @pl.loop(1, n_dp)
    def _(i):
        u = lax.rem(v + i, n_dp)
        peer_copy(cols.at[u], cols.at[u], c_send.at[u], g_recv.at[n * n_dp + u], k, dp=u).wait()

    out_total = jnp.zeros((1, rh), F32)
    bias_sums = []
    for u in range(n_dp):
        summed_bias = jnp.zeros((1, rh), F32)
        for j in range(n):
            got = gmsg[u * n + j]
            hid[(u * n + j) * FRESH : (u * n + j + 1) * FRESH, :] = got[0:FRESH]
            summed_bias = summed_bias + jnp.sum(got[0:FRESH], axis=0, keepdims=True)
            out_total = out_total + got[FRESH : FRESH + 1]
        bias_sums.append((gmsg[u * n, FRESH + 1 : FRESH + 2, :], summed_bias))
    cols_all = cols[...].reshape(n_dp * rows, cols_n)
    in_grad_ref[...] = dot_tn(cols_all, hid[...].astype(BF16))
    put_in = pltpu.make_async_copy(in_grad_ref, in_grad_hbm, out_sem.at[1])
    put_in.start()
    step_all = lax.broadcasted_iota(jnp.int32, bias_grad_ref.shape, 0).astype(F32)
    bias_total = jnp.zeros(bias_grad_ref.shape, F32)
    for at, summed_bias in bias_sums:
        bias_total = bias_total + jnp.where(step_all == at[None], summed_bias[None], 0.0)
    bias_grad_ref[...] = bias_total
    out_grad_ref[...] = out_total
    put_bias = pltpu.make_async_copy(bias_grad_ref, bias_grad_hbm, out_sem.at[2])
    put_out = pltpu.make_async_copy(out_grad_ref, out_grad_hbm, out_sem.at[3])
    put_bias.start()
    put_out.start()

    @pl.when(is1)
    def _():
        @pl.loop(0, n * n_dp)
        def _(t):
            peer_copy(
                gfirst,
                gmsg.at[t],
                g_send.at[n * n_dp + t],
                g_recv.at[t],
                lax.rem(t, n),
                pipe=0,
                dp=t // n,
            ).wait_send()

    pltpu.make_async_copy(blend, blended_hbm, out_sem.at[0]).wait()
    put_in.wait()
    put_bias.wait()
    put_out.wait()


def put_kernel(*refs):
    count = (len(refs) - 2) // 3
    sources, targets, held = refs[:count], refs[count : 2 * count], refs[2 * count : 3 * count]
    take_sems, put_sems = refs[-2:]
    parts = [
        (i, pl.ds(c * (sources[i].shape[0] // cuts), sources[i].shape[0] // cuts))
        for i in range(count)
        for cuts in [2 if i == 0 else 1]
        for c in range(cuts)
    ]
    takes = [
        pltpu.make_async_copy(sources[i].at[part], held[i].at[part], take_sems.at[s])
        for s, (i, part) in enumerate(parts)
    ]
    puts = [
        pltpu.make_async_copy(held[i].at[part], targets[i].at[part], put_sems.at[s])
        for s, (i, part) in enumerate(parts)
    ]
    for take in takes:
        take.start()
    for take, put in zip(takes, puts):
        take.wait()
        put.start()
    for put in puts:
        put.wait()


def body(
    n,
    n_dp,
    video_tokens,
    cached_out,
    fresh_mask,
    timestep,
    up_weight,
    down_weight,
    router_in,
    router_bias,
    router_out,
    out_cotangent,
):
    toks, dim = video_tokens.shape[1:]
    hidden = up_weight.shape[1]
    cols_n, rh = router_in.shape[1:]
    steps = router_bias.shape[1]
    rows = n * FRESH
    hbm = pl.BlockSpec(memory_space=pl.ANY)
    smem = pl.BlockSpec(memory_space=pltpu.SMEM)
    dma = pltpu.SemaphoreType.DMA
    shapes = (
        jax.ShapeDtypeStruct((toks, dim), BF16),
        jax.ShapeDtypeStruct((cols_n, rh), F32),
        jax.ShapeDtypeStruct((steps, 1, rh), F32),
        jax.ShapeDtypeStruct((1, rh), F32),
    )
    outs = pl.pallas_call(
        functools.partial(kernel, n, n_dp),
        out_shape=shapes,
        in_specs=[hbm, hbm, hbm, smem] + [hbm] * 6,
        out_specs=(hbm,) * 4,
        scratch_shapes=[
            pltpu.VMEM((hidden, dim), BF16),
            pltpu.VMEM((hidden, dim), BF16),
            pltpu.VMEM((toks, dim), BF16),
            pltpu.VMEM((toks, dim), BF16),
            pltpu.VMEM((toks, dim), BF16),
            pltpu.VMEM((1, toks), jnp.int32),
            pltpu.VMEM((cols_n, rh), BF16),
            pltpu.VMEM((steps, 1, rh), F32),
            pltpu.VMEM((1, rh), F32),
            pltpu.VMEM((cols_n, rh), F32),
            pltpu.VMEM((steps, 1, rh), F32),
            pltpu.VMEM((1, rh), F32),
            pltpu.VMEM((8, toks), F32),
            pltpu.VMEM((8, toks), F32),
            pltpu.VMEM((n, FRESH, dim), BF16),
            pltpu.VMEM((n, FRESH, dim), BF16),
            pltpu.VMEM((n, FRESH, dim), BF16),
            pltpu.VMEM((FRESH, dim), BF16),
            pltpu.VMEM((FRESH, dim), BF16),
            pltpu.VMEM((rows, dim), F32),
            pltpu.VMEM((rows, dim), F32),
            pltpu.VMEM((rows, rh + 128), F32),
            pltpu.VMEM((rows, hidden), F32),
            pltpu.VMEM((rows, hidden), F32),
            pltpu.VMEM((n, FRESH, dim + rh), BF16),
            pltpu.VMEM((n, FRESH, dim + rh), BF16),
            pltpu.VMEM((n, FRESH, rh + 128), F32),
            pltpu.VMEM((n, FRESH, rh + 128), F32),
            pltpu.VMEM((FRESH, dim), F32),
            pltpu.VMEM((FRESH, dim), F32),
            pltpu.VMEM((2 * FRESH, rh), F32),
            pltpu.VMEM((2 * FRESH, rh), F32),
            pltpu.VMEM((n_dp, rows, cols_n), BF16),
            pltpu.VMEM((n * n_dp, FRESH + 2, rh), F32),
            pltpu.VMEM((FRESH + 2, rh), F32),
            pltpu.VMEM((n_dp * rows, rh), F32),
            dma((8,)),
            dma((2,)),
            dma((n,)),
            dma((n,)),
            dma((n,)),
            dma((n,)),
            dma((n,)),
            dma((n,)),
            dma((n,)),
            dma((n,)),
            dma((4,)),
            dma((n,)),
            dma((n_dp,)),
            dma((n,)),
            dma((2 * n * n_dp,)),
            dma((n * n_dp + n_dp,)),
            dma((4,)),
        ],
        compiler_params=pltpu.CompilerParams(
            collective_id=0, has_side_effects=True, vmem_limit_bytes=67043328
        ),
    )(
        video_tokens[0],
        cached_out[0, 0],
        fresh_mask[0],
        timestep,
        up_weight[0],
        down_weight[0],
        router_in[0],
        jnp.transpose(router_bias, (1, 0, 2)),
        router_out,
        out_cotangent[0],
    )
    blended, in_grad, bias_grad, out_grad = pl.pallas_call(
        put_kernel,
        out_shape=shapes,
        in_specs=[hbm] * 4,
        out_specs=(hbm,) * 4,
        scratch_shapes=[pltpu.VMEM(shape.shape, shape.dtype) for shape in shapes]
        + [dma((5,)), dma((5,))],
        compiler_params=pltpu.CompilerParams(vmem_limit_bytes=67043328),
    )(*outs)
    return (blended[None, None], in_grad[None], jnp.transpose(bias_grad, (1, 0, 2)), out_grad)


def solution(mesh):
    placed = (
        P("dp", "fsdp", None),
        P("pipe", "dp", "fsdp", None),
        P("pipe", "dp", "fsdp"),
        P("dp"),
        P("pipe", "fsdp", None),
        P("pipe", "fsdp", None),
        P("pipe", "fsdp", None),
        P("pipe", None, None),
        P("pipe", None),
        P("dp", "fsdp", None),
    )
    return jax.shard_map(
        functools.partial(body, mesh.shape["fsdp"], mesh.shape["dp"]),
        mesh=mesh,
        in_specs=placed,
        out_specs=(
            P("pipe", "dp", "fsdp", None),
            P("pipe", "fsdp", None),
            P("pipe", None, None),
            P("pipe", None),
        ),
        check_vma=False,
    )
```

```python
import functools

import jax
import jax.numpy as jnp
from jax import lax
from jax.experimental import pallas as pl
from jax.experimental.pallas import tpu as pltpu
from jax.sharding import PartitionSpec as P

FRESH = 2

layer_eps = 1e-06
gelu_scale = 0.7978845608028654
gelu_cubic = 0.044715
F32 = jnp.float32
BF16 = jnp.bfloat16
MESH = pl.DeviceIdType.MESH


def gelu_both(values):
    inner_arg = gelu_scale * (values + gelu_cubic * values * values * values)
    tanh_val = jnp.tanh(inner_arg)
    gelu = 0.5 * values * (1.0 + tanh_val)
    slope = 0.5 * (1.0 + tanh_val) + 0.5 * values * (1.0 - tanh_val * tanh_val) * gelu_scale * (
        1.0 + 3.0 * gelu_cubic * values * values
    )
    return gelu, slope


def normalize(values):
    center = values - jnp.mean(values, axis=1, keepdims=True)
    inv_std = lax.rsqrt(jnp.mean(center * center, axis=1, keepdims=True) + layer_eps)
    return center * inv_std, inv_std


def normalize_back(scaled, inv_std, grads):
    return inv_std * (
        grads
        - jnp.mean(grads, axis=1, keepdims=True)
        - scaled * jnp.mean(grads * scaled, axis=1, keepdims=True)
    )


def dot_nn(left, right):
    return jnp.dot(left, right, preferred_element_type=F32)


def dot_nt(left, right):
    return lax.dot_general(left, right, (((1,), (1,)), ((), ())), preferred_element_type=F32)


def dot_tn(left, right):
    return lax.dot_general(left, right, (((0,), (0,)), ((), ())), preferred_element_type=F32)


def kernel(
    n,
    n_dp,
    tokens_hbm,
    cached_hbm,
    mask_hbm,
    step_ref,
    up_hbm,
    down_hbm,
    rin_hbm,
    bias_hbm,
    rout_hbm,
    cot_hbm,
    blended_hbm,
    in_grad_hbm,
    bias_grad_hbm,
    out_grad_hbm,
    up,
    down,
    first,
    cached,
    blend,
    mask_ref,
    rin_ref,
    bias_ref,
    rout_ref,
    in_grad_ref,
    bias_grad_ref,
    out_grad_ref,
    sel,
    psel,
    xin,
    win,
    cin,
    in1,
    w1,
    x32,
    c32,
    part_s,
    slope_ref,
    act_grad,
    send1,
    recv1,
    send2,
    recv2,
    delta,
    delta_in,
    factors,
    factors_in,
    cols,
    gmsg,
    gfirst,
    hid,
    load_sem,
    sel_sems,
    x_send,
    x_recv,
    w_send,
    w_recv,
    r1_send,
    r1_recv,
    r2_send,
    r2_recv,
    aux_sems,
    f_send,
    c_send,
    c_recv,
    g_send,
    g_recv,
    out_sem,
):
    k = lax.axis_index("fsdp")
    p = lax.axis_index("pipe")
    v = lax.axis_index("dp")
    is0 = p == 0
    is1 = p == 1
    dim = up.shape[1]
    rh = rin_ref.shape[1]
    cols_n = rin_ref.shape[0]
    rows = n * FRESH
    toward = 2 * ((2 * k) // n) - 1

    def ring(i):
        return lax.rem(k + n + toward * i, n)

    def ring_all(i):
        return ring(i // n_dp + 1), lax.rem(v + 1 + lax.rem(i, n_dp), n_dp)

    load_mask = pltpu.make_async_copy(mask_hbm, mask_ref, load_sem.at[0])
    load_rows = pltpu.make_async_copy(tokens_hbm, first, load_sem.at[1])
    load_cot = pltpu.make_async_copy(cot_hbm, first, load_sem.at[1])
    later = [
        pltpu.make_async_copy(cached_hbm, cached, load_sem.at[2]),
        pltpu.make_async_copy(up_hbm, up, load_sem.at[3]),
        pltpu.make_async_copy(down_hbm, down, load_sem.at[4]),
        pltpu.make_async_copy(rin_hbm, rin_ref, load_sem.at[5]),
        pltpu.make_async_copy(bias_hbm, bias_ref, load_sem.at[6]),
        pltpu.make_async_copy(rout_hbm, rout_ref, load_sem.at[7]),
    ]
    load_mask.start()

    @pl.when(is0)
    def _():
        load_rows.start()

    @pl.when(is1)
    def _():
        load_cot.start()

    barrier = pltpu.get_barrier_semaphore()
    count = n * 2 * n_dp
    flat = (k * 2 + p) * n_dp + v

    @pl.loop(1, count)
    def _(i):
        other = lax.rem(flat + i, count)
        pl.semaphore_signal(
            barrier,
            inc=1,
            device_id={
                "fsdp": other // (2 * n_dp),
                "pipe": lax.rem(other // n_dp, 2),
                "dp": lax.rem(other, n_dp),
            },
            device_id_type=MESH,
        )

    for load in later:
        load.start()

    load_mask.wait()
    toks = mask_ref.shape[1]
    lane = lax.broadcasted_iota(jnp.int32, (1, toks), 1).astype(F32)
    fresh = mask_ref[...] > 0
    low = jnp.min(jnp.where(fresh, lane, float(toks)), axis=1, keepdims=True)
    high = jnp.max(jnp.where(fresh, lane, -1.0), axis=1, keepdims=True)
    hot_low = jnp.where(lane == low, 1.0, 0.0)
    hot_high = jnp.where(jnp.logical_and(lane == high, high > low), 1.0, 0.0)
    row8 = lax.broadcasted_iota(jnp.int32, (8, toks), 0)
    hot = jnp.where(row8 == 0, hot_low, jnp.where(row8 == 1, hot_high, 0.0))
    sel[...] = hot
    hot_b = hot.astype(BF16)
    live = jnp.sum(hot, axis=1, keepdims=True)[:FRESH]

    load_rows.wait()
    picked = dot_nn(hot_b, first[...])[:FRESH]

    @pl.when(is0)
    def _():
        xin[k] = picked.astype(BF16)

    @pl.when(is1)
    def _():
        cin[k] = picked.astype(BF16)

    pl.semaphore_wait(barrier, count - 1)

    def peer_copy(src, dst, send_sem, recv_sem, j, **where):
        return pltpu.make_async_remote_copy(
            src_ref=src,
            dst_ref=dst,
            send_sem=send_sem,
            recv_sem=recv_sem,
            device_id={"fsdp": j, "pipe": p, "dp": v, **where},
            device_id_type=MESH,
        )

    @pl.when(is0)
    def _():
        @pl.loop(1, n)
        def _(i):
            j = ring(i)
            peer_copy(xin.at[k], xin.at[k], x_send.at[j], x_recv.at[k], j).start()

    @pl.when(is1)
    def _():
        @pl.loop(1, n)
        def _(i):
            j = ring(i)
            peer_copy(cin.at[k], cin.at[k], x_send.at[j], c_recv.at[k], j).start()

    sel_copy = peer_copy(sel, psel, sel_sems.at[0], sel_sems.at[1], k, pipe=1 - p)
    sel_copy.start()
    for load in later:
        load.wait()
    cached_rows = dot_nn(hot_b, cached[...])[:FRESH]
    sel_copy.wait()
    other_hot = psel[...]
    same_0 = jnp.sum(other_hot[:FRESH] * hot[0:1], axis=1, keepdims=True)
    same_1 = jnp.sum(other_hot[:FRESH] * hot[1:2], axis=1, keepdims=True)
    other_rows = dot_nn(other_hot.astype(BF16), cached[...])[:FRESH]
    step_val = jnp.full((1, rh), step_ref[0], jnp.int32)
    bias_row = bias_ref[step_ref[0]]
    r_out = rout_ref[...]

    @pl.when(is0)
    def _():
        @pl.loop(1, n)
        def _(i):
            j = lax.rem(k + i, n)
            peer_copy(xin.at[j], xin.at[j], x_send.at[j], x_recv.at[j], j).wait()

    @pl.when(is1)
    def _():
        @pl.loop(1, n)
        def _(i):
            j = lax.rem(k + i, n)
            peer_copy(cin.at[j], cin.at[j], x_send.at[j], c_recv.at[j], j).wait()

        for j in range(n):
            c32[j * FRESH : (j + 1) * FRESH, :] = cin[j].astype(F32)
        act_grad[...] = dot_nt(c32[...].astype(BF16), down[...])

        @pl.loop(0, n)
        def _(j):
            peer_copy(xin.at[j], xin.at[j], x_send.at[j], x_recv.at[j], j, pipe=0).wait_recv()

    for j in range(n):
        x32[j * FRESH : (j + 1) * FRESH, :] = xin[j].astype(F32)
    scaled_all, _ = normalize(x32[...])
    x32[...] = scaled_all
    normed = scaled_all.astype(BF16)
    for j in range(n):

        @pl.when(k == j)
        def _():
            cols[v] = x32[:, j * cols_n : (j + 1) * cols_n].astype(BF16)

    router_part = dot_nn(cols[v], rin_ref[...])
    pre_act = dot_nt(normed, up[...])
    act, slope = gelu_both(pre_act)
    slope_ref[...] = slope
    term = dot_nn(act.astype(BF16), down[...])
    for j in range(n):
        send1[j, :, :dim] = term[j * FRESH : (j + 1) * FRESH].astype(BF16)
        send1[j, :, dim:] = router_part[j * FRESH : (j + 1) * FRESH].astype(BF16)

    @pl.loop(1, n)
    def _(i):
        j = ring(i)
        peer_copy(send1.at[j], recv1.at[k], r1_send.at[j], r1_recv.at[k], j).start()

    @pl.when(is1)
    def _():
        @pl.loop(0, n)
        def _(j):
            peer_copy(win.at[j], win.at[j], x_send.at[j], w_recv.at[j], j, pipe=0).wait_recv()

        for j in range(n):
            c32[j * FRESH : (j + 1) * FRESH, :] = win[j].astype(F32)
        for j in range(n):

            @pl.when(k == j)
            def _():
                part_s[:, 0:rh] = dot_nn(
                    c32[:, j * cols_n : (j + 1) * cols_n].astype(BF16), rin_ref[...]
                )

        up_w = dot_nt(c32[...].astype(BF16), up[...])
        along = jnp.sum(act_grad[...] * slope_ref[...] * up_w, axis=1, keepdims=True)
        part_s[:, rh:] = jnp.broadcast_to(along, (rows, part_s.shape[1] - rh))
        for j in range(n):
            send2[j] = part_s[j * FRESH : (j + 1) * FRESH, :]

        @pl.loop(1, n)
        def _(i):
            j = ring(i)
            peer_copy(send2.at[j], recv2.at[k], r2_send.at[j], r2_recv.at[k], j).start()

        recv2[k] = send2[k]

    recv1[k] = send1[k]

    @pl.loop(1, n_dp)
    def _(i):
        u = lax.rem(v + i, n_dp)
        peer_copy(cols.at[v], cols.at[v], c_send.at[u], g_recv.at[n * n_dp + v], k, dp=u).start()

    own_in = xin[k].astype(F32)

    @pl.loop(1, n)
    def _(i):
        j = lax.rem(k + i, n)
        peer_copy(send1.at[j], recv1.at[j], r1_send.at[j], r1_recv.at[j], j).wait()

    summed = recv1[0].astype(F32)
    for j in range(1, n):
        summed = summed + recv1[j].astype(F32)
    fresh_out = own_in + summed[:, :dim]
    router_pre = summed[:, dim:] + bias_row
    router_act, router_slope = gelu_both(router_pre)
    gate = jax.nn.sigmoid(jnp.sum(router_act * r_out, axis=1, keepdims=True))
    gap = live * (fresh_out - cached_rows)
    new_rows = (cached_rows + gate * gap).astype(BF16).astype(F32)
    gate_slope = gate * (1.0 - gate)
    hid_factor = gate_slope * r_out * router_slope
    out_factor = gate_slope * router_act

    def blend_out():
        turned = jnp.transpose(hot)
        kept = cached[...].astype(F32)
        mixed = jnp.where(
            turned[:, 0:1] > 0.5,
            new_rows[0:1],
            jnp.where(turned[:, 1:2] > 0.5, new_rows[1:2], kept),
        )
        blend[...] = mixed.astype(BF16)
        pltpu.make_async_copy(blend, blended_hbm, out_sem.at[0]).start()

    slot = v * n + k
    delta_copy = peer_copy(delta, delta_in, aux_sems.at[0], aux_sems.at[1], k, pipe=1 - p)
    factor_copy = peer_copy(factors, factors_in, aux_sems.at[2], aux_sems.at[3], k, pipe=1 - p)

    @pl.when(is0)
    def _():
        moved = jnp.where(
            same_0 > 0.5, new_rows[0:1], jnp.where(same_1 > 0.5, new_rows[1:2], other_rows)
        )
        in1[...] = moved.astype(BF16)

        @pl.loop(0, n)
        def _(i):
            j = ring(i + 1)
            peer_copy(in1, xin.at[k], f_send.at[j], x_recv.at[k], j, pipe=1).start()

        met = same_0 * gap[0:1] + same_1 * gap[1:2]
        scaled, inv_std = normalize(moved)
        w1[...] = normalize_back(scaled, inv_std, met).astype(BF16)

        @pl.loop(0, n)
        def _(j):
            peer_copy(in1, xin.at[j], f_send.at[j], x_recv.at[j], j, pipe=1).wait_send()

        @pl.loop(0, n)
        def _(i):
            j = ring(i + 1)
            peer_copy(w1, win.at[k], w_send.at[j], w_recv.at[k], j, pipe=1).start()

        delta[...] = met
        factors[0:FRESH, :] = hid_factor
        factors[FRESH : 2 * FRESH, :] = out_factor
        delta_copy.start()
        factor_copy.start()
        blend_out()

        @pl.loop(0, n)
        def _(j):
            peer_copy(w1, win.at[j], w_send.at[j], w_recv.at[j], j, pipe=1).wait_send()

        delta_copy.wait_send()
        factor_copy.wait_send()

        @pl.loop(0, n * n_dp)
        def _(j):
            peer_copy(
                gmsg.at[j], gmsg.at[j], g_send.at[j], g_recv.at[j], k, pipe=1
            ).wait_recv()

    def message(ref, gate_grad, hid_fac, out_fac):
        ref[0:FRESH, :] = gate_grad * hid_fac
        ref[FRESH : FRESH + 1, :] = jnp.sum(gate_grad * out_fac, axis=0, keepdims=True)
        ref[FRESH + 1 : FRESH + 2, :] = step_val.astype(F32)

    @pl.when(is1)
    def _():
        gate_grad = jnp.sum(picked * gap, axis=1, keepdims=True)
        message(gmsg.at[slot], gate_grad, hid_factor, out_factor)

        delta_copy.wait_recv()
        factor_copy.wait_recv()
        straight = jnp.sum(picked * delta_in[...], axis=1, keepdims=True)

        @pl.loop(1, n)
        def _(i):
            j = lax.rem(k + i, n)
            peer_copy(send2.at[j], recv2.at[j], r2_send.at[j], r2_recv.at[j], j).wait()

        through = recv2[0]
        for j in range(1, n):
            through = through + recv2[j]
        met_grad = live * gate * (straight + through[:, rh : rh + 1]) + jnp.sum(
            gate_grad * hid_factor * through[:, 0:rh], axis=1, keepdims=True
        )
        gate_grad_first = same_0 * met_grad[0:1] + same_1 * met_grad[1:2]
        message(
            gfirst,
            gate_grad_first,
            factors_in[0:FRESH, :],
            factors_in[FRESH : 2 * FRESH, :],
        )

        @pl.loop(0, n * n_dp)
        def _(i):
            j, u = ring_all(i)
            peer_copy(
                gfirst,
                gmsg.at[slot],
                g_send.at[n * n_dp + u * n + j],
                g_recv.at[slot],
                j,
                pipe=0,
                dp=u,
            ).start()

        @pl.loop(0, n * n_dp - 1)
        def _(i):
            j, u = ring_all(i)
            peer_copy(
                gmsg.at[slot], gmsg.at[slot], g_send.at[u * n + j], g_recv.at[slot], j, dp=u
            ).start()

        blend_out()

        @pl.loop(1, n * n_dp)
        def _(i):
            t = lax.rem(slot + i, n * n_dp)
            peer_copy(
                gmsg.at[t], gmsg.at[t], g_send.at[t], g_recv.at[t], lax.rem(t, n), dp=t // n
            ).wait()

    @pl.loop(1, n_dp)
    def _(i):
        u = lax.rem(v + i, n_dp)
        peer_copy(cols.at[u], cols.at[u], c_send.at[u], g_recv.at[n * n_dp + u], k, dp=u).wait()

    out_total = jnp.zeros((1, rh), F32)
    bias_sums = []
    for u in range(n_dp):
        summed_bias = jnp.zeros((1, rh), F32)
        for j in range(n):
            got = gmsg[u * n + j]
            hid[(u * n + j) * FRESH : (u * n + j + 1) * FRESH, :] = got[0:FRESH]
            summed_bias = summed_bias + jnp.sum(got[0:FRESH], axis=0, keepdims=True)
            out_total = out_total + got[FRESH : FRESH + 1]
        bias_sums.append((gmsg[u * n, FRESH + 1 : FRESH + 2, :], summed_bias))
    cols_all = cols[...].reshape(n_dp * rows, cols_n)
    in_grad_ref[...] = dot_tn(cols_all, hid[...].astype(BF16))
    put_in = pltpu.make_async_copy(in_grad_ref, in_grad_hbm, out_sem.at[1])
    put_in.start()
    step_all = lax.broadcasted_iota(jnp.int32, bias_grad_ref.shape, 0).astype(F32)
    bias_total = jnp.zeros(bias_grad_ref.shape, F32)
    for at, summed_bias in bias_sums:
        bias_total = bias_total + jnp.where(step_all == at[None], summed_bias[None], 0.0)
    bias_grad_ref[...] = bias_total
    out_grad_ref[...] = out_total
    put_bias = pltpu.make_async_copy(bias_grad_ref, bias_grad_hbm, out_sem.at[2])
    put_out = pltpu.make_async_copy(out_grad_ref, out_grad_hbm, out_sem.at[3])
    put_bias.start()
    put_out.start()

    @pl.when(is1)
    def _():
        @pl.loop(0, n * n_dp)
        def _(t):
            peer_copy(
                gfirst,
                gmsg.at[t],
                g_send.at[n * n_dp + t],
                g_recv.at[t],
                lax.rem(t, n),
                pipe=0,
                dp=t // n,
            ).wait_send()

    pltpu.make_async_copy(blend, blended_hbm, out_sem.at[0]).wait()
    put_in.wait()
    put_bias.wait()
    put_out.wait()


def put_kernel(*refs):
    count = (len(refs) - 2) // 3
    sources, targets, held = refs[:count], refs[count : 2 * count], refs[2 * count : 3 * count]
    take_sems, put_sems = refs[-2:]
    parts = [
        (i, pl.ds(c * (sources[i].shape[0] // cuts), sources[i].shape[0] // cuts))
        for i in range(count)
        for cuts in [2 if i == 0 else 1]
        for c in range(cuts)
    ]
    takes = [
        pltpu.make_async_copy(sources[i].at[part], held[i].at[part], take_sems.at[s])
        for s, (i, part) in enumerate(parts)
    ]
    puts = [
        pltpu.make_async_copy(held[i].at[part], targets[i].at[part], put_sems.at[s])
        for s, (i, part) in enumerate(parts)
    ]
    for take in takes:
        take.start()
    for take, put in zip(takes, puts):
        take.wait()
        put.start()
    for put in puts:
        put.wait()


def body(
    n,
    n_dp,
    video_tokens,
    cached_out,
    fresh_mask,
    timestep,
    up_weight,
    down_weight,
    router_in,
    router_bias,
    router_out,
    out_cotangent,
):
    toks, dim = video_tokens.shape[1:]
    hidden = up_weight.shape[1]
    cols_n, rh = router_in.shape[1:]
    steps = router_bias.shape[1]
    rows = n * FRESH
    hbm = pl.BlockSpec(memory_space=pl.ANY)
    smem = pl.BlockSpec(memory_space=pltpu.SMEM)
    dma = pltpu.SemaphoreType.DMA
    shapes = (
        jax.ShapeDtypeStruct((toks, dim), BF16),
        jax.ShapeDtypeStruct((cols_n, rh), F32),
        jax.ShapeDtypeStruct((steps, 1, rh), F32),
        jax.ShapeDtypeStruct((1, rh), F32),
    )
    outs = pl.pallas_call(
        functools.partial(kernel, n, n_dp),
        out_shape=shapes,
        in_specs=[hbm, hbm, hbm, smem] + [hbm] * 6,
        out_specs=(hbm,) * 4,
        scratch_shapes=[
            pltpu.VMEM((hidden, dim), BF16),
            pltpu.VMEM((hidden, dim), BF16),
            pltpu.VMEM((toks, dim), BF16),
            pltpu.VMEM((toks, dim), BF16),
            pltpu.VMEM((toks, dim), BF16),
            pltpu.VMEM((1, toks), jnp.int32),
            pltpu.VMEM((cols_n, rh), BF16),
            pltpu.VMEM((steps, 1, rh), F32),
            pltpu.VMEM((1, rh), F32),
            pltpu.VMEM((cols_n, rh), F32),
            pltpu.VMEM((steps, 1, rh), F32),
            pltpu.VMEM((1, rh), F32),
            pltpu.VMEM((8, toks), F32),
            pltpu.VMEM((8, toks), F32),
            pltpu.VMEM((n, FRESH, dim), BF16),
            pltpu.VMEM((n, FRESH, dim), BF16),
            pltpu.VMEM((n, FRESH, dim), BF16),
            pltpu.VMEM((FRESH, dim), BF16),
            pltpu.VMEM((FRESH, dim), BF16),
            pltpu.VMEM((rows, dim), F32),
            pltpu.VMEM((rows, dim), F32),
            pltpu.VMEM((rows, rh + 128), F32),
            pltpu.VMEM((rows, hidden), F32),
            pltpu.VMEM((rows, hidden), F32),
            pltpu.VMEM((n, FRESH, dim + rh), BF16),
            pltpu.VMEM((n, FRESH, dim + rh), BF16),
            pltpu.VMEM((n, FRESH, rh + 128), F32),
            pltpu.VMEM((n, FRESH, rh + 128), F32),
            pltpu.VMEM((FRESH, dim), F32),
            pltpu.VMEM((FRESH, dim), F32),
            pltpu.VMEM((2 * FRESH, rh), F32),
            pltpu.VMEM((2 * FRESH, rh), F32),
            pltpu.VMEM((n_dp, rows, cols_n), BF16),
            pltpu.VMEM((n * n_dp, FRESH + 2, rh), F32),
            pltpu.VMEM((FRESH + 2, rh), F32),
            pltpu.VMEM((n_dp * rows, rh), F32),
            dma((8,)),
            dma((2,)),
            dma((n,)),
            dma((n,)),
            dma((n,)),
            dma((n,)),
            dma((n,)),
            dma((n,)),
            dma((n,)),
            dma((n,)),
            dma((4,)),
            dma((n,)),
            dma((n_dp,)),
            dma((n,)),
            dma((2 * n * n_dp,)),
            dma((n * n_dp + n_dp,)),
            dma((4,)),
        ],
        compiler_params=pltpu.CompilerParams(
            collective_id=0, has_side_effects=True, vmem_limit_bytes=67043328
        ),
    )(
        video_tokens[0],
        cached_out[0, 0],
        fresh_mask[0],
        timestep,
        up_weight[0],
        down_weight[0],
        router_in[0],
        jnp.transpose(router_bias, (1, 0, 2)),
        router_out,
        out_cotangent[0],
    )
    blended, in_grad, bias_grad, out_grad = pl.pallas_call(
        put_kernel,
        out_shape=shapes,
        in_specs=[hbm] * 4,
        out_specs=(hbm,) * 4,
        scratch_shapes=[pltpu.VMEM(shape.shape, shape.dtype) for shape in shapes]
        + [dma((5,)), dma((5,))],
        compiler_params=pltpu.CompilerParams(vmem_limit_bytes=67043328),
    )(*outs)
    return (blended[None, None], in_grad[None], jnp.transpose(bias_grad, (1, 0, 2)), out_grad)


def solution(mesh):
    placed = (
        P("dp", "fsdp", None),
        P("pipe", "dp", "fsdp", None),
        P("pipe", "dp", "fsdp"),
        P("dp"),
        P("pipe", "fsdp", None),
        P("pipe", "fsdp", None),
        P("pipe", "fsdp", None),
        P("pipe", None, None),
        P("pipe", None),
        P("dp", "fsdp", None),
    )
    return jax.shard_map(
        functools.partial(body, mesh.shape["fsdp"], mesh.shape["dp"]),
        mesh=mesh,
        in_specs=placed,
        out_specs=(
            P("pipe", "dp", "fsdp", None),
            P("pipe", "fsdp", None),
            P("pipe", None, None),
            P("pipe", None),
        ),
        check_vma=False,
    )
```
